256 devices in a mesh: temp: 8 (over y, core), dom: 32 (over x, z).
Axes of the slice: x: 4, y: 4, z: 8, core: 2. Of those that a mesh axis runs over, the one named last changes fastest.
Arguments:
- particles: bfloat16 [8, 16384, 3072], P('temp', 'dom'), may hold values from -6 to 6
- log_weights: float32 [8, 16384], P('temp', 'dom'), may hold values from -200 to 200
- offspring: int32 [8, 256], P('temp', 'dom'), may hold values from 0 to 2, as said below
- even_pairs: int32 [8, 256], P('temp', 'dom'), may hold values from 0 to 1, as said below
- odd_pairs: int32 [8, 256], P('temp', 'dom'), may hold values from 0 to 1, as said below
- inverse_temp: float32 [8], P('temp'), may hold values from 0.5 to 4
- flow_in: bfloat16 [1536, 512], replicated, may hold values from -0.15625 to 0.15625
- flow_mid: bfloat16 [512, 512], replicated, may hold values from -0.25 to 0.25
- flow_out: bfloat16 [512, 3072], replicated, may hold values from -0.25 to 0.25
- energy_in: bfloat16 [3072, 512], replicated, may hold values from -0.109375 to 0.109375
- energy_mid: bfloat16 [512, 512], replicated, may hold values from -0.25 to 0.25
- energy_out: float32 [512], replicated, may hold values from -0.25 to 0.25
Outputs:
- new_particles: bfloat16 [8, 16384, 3072], P('temp', 'dom')
- new_log_weights: float32 [8, 16384], P('temp', 'dom')
- log_ess: float32 [8], P('temp')
The draws below stay inside these ranges and needn't reach their ends.
Inputs may be any that keep to these rules, and one draw needn't show every extreme that they name: `offspring`: counts are 0, 1 or 2 and each group's counts sum to 256. Of the 8 blocks of one device at most 1 have count 2 and at most 1 have count 0; in every group some device has exactly 1 with count 2 and some device exactly 1 with count 0. `even_pairs`: groups 2i and 2i + 1 carry equal rows. At most 2 of the 8 blocks of one device are 1, and in every pair some device has exactly 2. `odd_pairs`: groups 2i + 1 and 2i + 2 carry equal rows; groups 0 and 7 are all 0. At most 2 of the 8 blocks of one device are 1, and in every pair some device has exactly 2.
All inputs are finite; a program needn't handle non-finite values.
Results may differ from the reference program's by a relative error of at most 0.0024.
Values may be sent and summed in bfloat16 or wider, within the bound.
No kernel may reach another device: no remote copies, remote signals or barrier semaphores. Data moves between devices by JAX's collectives and lax.ppermute only.
A program may use at most 128 MiB of HBM per device.

```python
import math
import jax
import jax.numpy as jnp
from jax import lax

DIM = 3072
HID = 512
SURPLUS = 1
SWAPS = 2
BLK_DEV = 8
GROUPS = 8
NBLK = 256
PARTICLES = 16384


def draw_log_weights(key, part):
    key_one = jax.random.fold_in(key, 0)
    position = jnp.arange(PARTICLES, dtype=jnp.float32) / (PARTICLES - 1)
    noise = jax.random.normal(key_one, (GROUPS, PARTICLES), jnp.float32)
    return (noise + jnp.log(1.0 + 2.0 * position)[None, :]).astype(jnp.float32)


def draw_offspring(key, part):
    devices = NBLK // BLK_DEV
    half_devices = devices // 2
    key_one, key_two, key_three, key_four, key_five, key_six = jax.random.split(key, 6)
    device_ids = jnp.arange(devices)
    surplus_rows = jax.random.randint(key_one, (GROUPS, devices), 0, SURPLUS + 1)
    forced = jax.random.randint(key_two, (GROUPS,), 0, half_devices)
    surplus_rows = jnp.where(device_ids[None, :] == forced[:, None], SURPLUS, surplus_rows)
    random_permute = jax.vmap(lambda subkey: jax.random.permutation(subkey, devices))(jax.random.split(key_three, GROUPS))
    mixed_empty = jnp.take_along_axis(surplus_rows, random_permute, axis=1)
    far_surplus = jnp.where(device_ids[None, :] < half_devices, surplus_rows, 0)
    far_empty = jnp.roll(far_surplus, half_devices, axis=1)
    chosen_group = jax.random.randint(key_six, (), 0, GROUPS)
    use_far = (jax.random.randint(key_five, (GROUPS,), 0, 2) == 1) | (jnp.arange(GROUPS) == chosen_group)
    spare_count = jnp.where(use_far[:, None], far_surplus, surplus_rows)
    empty_slots = jnp.where(use_far[:, None], far_empty, mixed_empty)
    rank_order = jax.vmap(lambda subkey: jax.random.permutation(subkey, BLK_DEV))(jax.random.split(key_four, GROUPS * devices))
    rank_order = rank_order.reshape(GROUPS, devices, BLK_DEV)
    doubled = rank_order < spare_count[:, :, None]
    discarded_rows = (rank_order >= spare_count[:, :, None]) & (rank_order < (spare_count + empty_slots)[:, :, None])
    counts = 1 + doubled.astype(jnp.int32) - discarded_rows.astype(jnp.int32)
    return counts.reshape(GROUPS, NBLK).astype(jnp.int32)


def pair_masks(key, pairs):
    devices = NBLK // BLK_DEV
    key_one, key_two, key_three = jax.random.split(key, 3)
    number = jax.random.randint(key_one, (pairs, devices), 0, SWAPS + 1)
    forced = jax.random.randint(key_two, (pairs,), 0, devices)
    number = jnp.where(jnp.arange(devices)[None, :] == forced[:, None], SWAPS, number)
    rank_order = jax.vmap(lambda subkey: jax.random.permutation(subkey, BLK_DEV))(jax.random.split(key_three, pairs * devices))
    rank_order = rank_order.reshape(pairs, devices, BLK_DEV)
    return (rank_order < number[:, :, None]).astype(jnp.int32).reshape(pairs, NBLK)


def draw_even_pairs(key, part):
    return jnp.repeat(pair_masks(jax.random.fold_in(key, 11), GROUPS // 2), 2, axis=0)


def draw_odd_pairs(key, part):
    inner = jnp.repeat(pair_masks(jax.random.fold_in(key, 23), GROUPS // 2 - 1), 2, axis=0)
    border = jnp.zeros((1, NBLK), jnp.int32)
    return jnp.concatenate([border, inner, border], axis=0)


def shard_levels(stream_key, shape, shards, least, high):
    factor_of, own = 1.0, jax.random.fold_in(stream_key, 6)
    for dim, shards_of in shards:
        steps = jnp.exp(jax.random.uniform(jax.random.fold_in(own, dim), (shards_of,), jnp.float32, least / len(shards), high / len(shards)))
        factor_of = factor_of * jnp.repeat(steps, shape[dim] // shards_of).reshape([-1 if axis == dim else 1 for axis in range(len(shape))])
    return factor_of


def centred(rng, dims, scale, limit, pieces=(), kind=jnp.bfloat16):
    drawn = scale * jax.random.normal(rng, dims, jnp.float32)
    if pieces:
        drawn = drawn * shard_levels(rng, dims, pieces, -0.22, 0.18)
    return jnp.clip(drawn, -limit, limit).astype(kind)


def setup_inputs(seed: int = 0) -> dict:
    key_of = jax.random.split(jax.random.key(seed), 13)
    particles = centred(key_of[0], (GROUPS, PARTICLES, DIM), 1.0, 6.0, ((0, 8), (1, 32)))
    log_weights = draw_log_weights(jax.random.fold_in(key_of[12], 71), 0)
    offspring = draw_offspring(jax.random.fold_in(key_of[12], 71), 0)
    even_pairs = draw_even_pairs(jax.random.fold_in(key_of[12], 71), 0)
    odd_pairs = draw_odd_pairs(jax.random.fold_in(key_of[12], 71), 0)
    inverse_temp = jnp.clip(jnp.exp(math.log(4.0) - 2.0794415 * jax.random.uniform(key_of[5], (GROUPS,), jnp.float32) ** shard_levels(key_of[5], (GROUPS,), ((0, 8),), -0.2, 0.2)), 0.5, 4.0)
    flow_in = centred(key_of[6], (DIM // 2, HID), (DIM // 2) ** -0.5, 0.15625)
    flow_mid = centred(key_of[7], (HID, HID), HID ** -0.5, 0.25)
    flow_out = centred(key_of[8], (HID, DIM), HID ** -0.5, 0.25)
    energy_in = centred(key_of[9], (DIM, HID), DIM ** -0.5, 0.109375)
    energy_mid = centred(key_of[10], (HID, HID), HID ** -0.5, 0.25)
    energy_out = centred(key_of[11], (HID,), HID ** -0.5, 0.25, (), jnp.float32)
    return dict(particles=particles, log_weights=log_weights, offspring=offspring, even_pairs=even_pairs, odd_pairs=odd_pairs, inverse_temp=inverse_temp, flow_in=flow_in, flow_mid=flow_mid, flow_out=flow_out, energy_in=energy_in, energy_mid=energy_mid, energy_out=energy_out)


old_level = 0.5
new_level = 0.75
scale_limit = 0.05


def transport(row_data, flow_in, flow_mid, flow_out):
    half_width = row_data.shape[1] // 2
    kept_half = row_data[:, :half_width]
    moved_half = row_data[:, half_width:]
    hidden_one = jax.nn.gelu(jnp.dot(kept_half, flow_in, preferred_element_type=jnp.float32)).astype(jnp.bfloat16)
    hidden_two = jax.nn.gelu(jnp.dot(hidden_one, flow_mid, preferred_element_type=jnp.float32)).astype(jnp.bfloat16)
    scale_shift = jnp.dot(hidden_two, flow_out, preferred_element_type=jnp.float32)
    log_scale = scale_limit * jnp.tanh(scale_shift[:, :half_width])
    offset_rows = (moved_half.astype(jnp.float32) * jnp.exp(log_scale) + scale_shift[:, half_width:]).astype(jnp.bfloat16)
    return jnp.concatenate([kept_half, offset_rows], axis=1), jnp.sum(log_scale, axis=1)


def energy(row_data, energy_in, energy_mid, energy_out):
    layer_one = jax.nn.gelu(jnp.dot(row_data, energy_in, preferred_element_type=jnp.float32)).astype(jnp.bfloat16)
    layer_two = jax.nn.gelu(jnp.dot(layer_one, energy_mid, preferred_element_type=jnp.float32))
    return jnp.sum(layer_two * energy_out[None, :], axis=1)


def resample_group(blocks, weights, counts):
    doubled = (counts == 2).astype(jnp.int32)
    discarded_rows = (counts == 0).astype(jnp.int32)
    spare_rank = jnp.cumsum(doubled) - 1
    vacant_rank = jnp.cumsum(discarded_rows) - 1
    positions = jnp.arange(counts.shape[0], dtype=jnp.int32)
    matches = (doubled[None, :] == 1) & (spare_rank[None, :] == vacant_rank[:, None])
    source = jnp.sum(jnp.where(matches, positions[None, :], 0), axis=1).astype(jnp.int32)
    weights = weights - jnp.log(jnp.maximum(counts, 1).astype(jnp.float32))[:, None]
    vacant = discarded_rows == 1
    blocks = jnp.where(vacant[:, None, None], jnp.take(blocks, source, axis=0), blocks)
    weights = jnp.where(vacant[:, None], jnp.take(weights, source, axis=0), weights)
    return blocks, weights


def reference(particles, log_weights, offspring, even_pairs, odd_pairs, inverse_temp, flow_in, flow_mid, flow_out, energy_in, energy_mid, energy_out):
    groups = particles.shape[0]
    block_count = offspring.shape[1]
    block_rows = particles.shape[1] // block_count
    features = particles.shape[2]
    blocks = particles.reshape(groups, block_count, block_rows, features)
    weights = log_weights.reshape(groups, block_count, block_rows)
    blocks, weights = jax.vmap(resample_group)(blocks, weights, offspring)
    group_ids = jnp.arange(groups, dtype=jnp.int32)
    even_partner = group_ids + 1 - 2 * (group_ids % 2)
    odd_partner = jnp.clip(group_ids - 1 + 2 * (group_ids % 2), 0, groups - 1)
    blocks = jnp.where((even_pairs == 1)[:, :, None, None], jnp.take(blocks, even_partner, axis=0), blocks)
    blocks = jnp.where((odd_pairs == 1)[:, :, None, None], jnp.take(blocks, odd_partner, axis=0), blocks)
    row_data = blocks.reshape(groups, block_count * block_rows, features)

    def per_group(item):
        rows_in = item
        moved, log_det = transport(rows_in, flow_in, flow_mid, flow_out)
        before = energy(rows_in, energy_in, energy_mid, energy_out)
        after = energy(moved, energy_in, energy_mid, energy_out)
        return moved, log_det, before, after

    moved, log_det, before, after = lax.map(per_group, row_data)
    updated = weights.reshape(groups, -1) + log_det - inverse_temp[:, None] * (new_level * after - old_level * before)
    peak = jnp.max(updated, axis=1)
    first_sum = jnp.sum(jnp.exp(updated - peak[:, None]), axis=1)
    second_sum = jnp.sum(jnp.exp(2.0 * (updated - peak[:, None])), axis=1)
    new_log_weights = updated - (peak + jnp.log(first_sum))[:, None]
    log_ess = 2.0 * jnp.log(first_sum) - jnp.log(second_sum) - jnp.log(jnp.float32(updated.shape[1]))
    return moved, new_log_weights, log_ess
```

```python
import jax
import jax.numpy as jnp
from jax import lax
from jax.sharding import PartitionSpec as P

SURPLUS = 1
SWAPS = 2


old_level = 0.5
new_level = 0.75
scale_limit = 0.05


def transport(row_data, flow_in, flow_mid, flow_out):
    half_width = row_data.shape[1] // 2
    kept_half = row_data[:, :half_width]
    moved_half = row_data[:, half_width:]
    hidden_one = jax.nn.gelu(
        jnp.dot(kept_half, flow_in, preferred_element_type=jnp.float32)
    ).astype(jnp.bfloat16)
    hidden_two = jax.nn.gelu(
        jnp.dot(hidden_one, flow_mid, preferred_element_type=jnp.float32)
    ).astype(jnp.bfloat16)
    scale_shift = jnp.dot(hidden_two, flow_out, preferred_element_type=jnp.float32)
    log_scale = scale_limit * jnp.tanh(scale_shift[:, :half_width])
    offset_rows = (
        moved_half.astype(jnp.float32) * jnp.exp(log_scale) + scale_shift[:, half_width:]
    ).astype(jnp.bfloat16)
    return (jnp.concatenate([kept_half, offset_rows], axis=1), jnp.sum(log_scale, axis=1))


def energy(row_data, energy_in, energy_mid, energy_out):
    layer_one = jax.nn.gelu(
        jnp.dot(row_data, energy_in, preferred_element_type=jnp.float32)
    ).astype(jnp.bfloat16)
    layer_two = jax.nn.gelu(jnp.dot(layer_one, energy_mid, preferred_element_type=jnp.float32))
    return jnp.sum(layer_two * energy_out[None, :], axis=1)


def pick_rows(flags, rank_order, slot_count):
    slot_ids = jnp.arange(slot_count, dtype=jnp.int32)
    positions = jnp.arange(flags.shape[0], dtype=jnp.int32)
    matches = (flags[None, :] == 1) & (rank_order[None, :] == slot_ids[:, None])
    return jnp.sum(jnp.where(matches, positions[None, :], 0), axis=1)


def broadcast_rows(row, count):
    stacked = jnp.broadcast_to(row[None], (count,) + row.shape)
    return lax.all_to_all(stacked, "dom", 0, 0, tiled=True)


def to_pieces(block):
    rows, features = block.shape
    cut = block.reshape(rows // 8, 8, 4, features // 4)
    return cut.transpose(0, 2, 1, 3).reshape(rows // 2, 8, features // 4)


def from_pieces(pieces):
    count, _, width = pieces.shape
    cut = pieces.reshape(count // 4, 4, 8, width)
    return cut.transpose(0, 2, 1, 3).reshape(count * 2, width * 4)


def neighbour_swap(blocks, swap_mask, pairs):
    rank_order = jnp.cumsum(swap_mask) - 1
    chosen = pick_rows(swap_mask, rank_order, SWAPS)
    packed = jnp.concatenate([lax.dynamic_slice_in_dim(blocks, chosen[i], 1) for i in range(SWAPS)])
    received = lax.ppermute(packed, "temp", pairs)
    for i in range(SWAPS):
        hit = (swap_mask == 1) & (rank_order == i)
        blocks = jnp.where(hit[:, None, None], received[i][None], blocks)
    return blocks


def per_device(
    particles,
    log_weights,
    offspring,
    even_pairs,
    odd_pairs,
    inverse_temp,
    flow_in,
    flow_mid,
    flow_out,
    energy_in,
    energy_mid,
    energy_out,
):
    block_count = offspring.shape[1]
    features = particles.shape[2]
    block_rows = particles.shape[1] // block_count
    spare_rows = SURPLUS * block_rows
    blocks = particles[0].reshape(block_count, block_rows, features)
    counts = offspring[0]
    doubled = (counts == 2).astype(jnp.int32)
    discarded_rows = (counts == 0).astype(jnp.int32)
    spare_rank = jnp.cumsum(doubled) - 1
    vacant_rank = jnp.cumsum(discarded_rows) - 1
    weights = (
        log_weights[0].reshape(block_count, block_rows)
        - jnp.log(jnp.maximum(counts, 1).astype(jnp.float32))[:, None]
    )
    spare_ids = pick_rows(doubled, spare_rank, SURPLUS)
    spare_blocks = jnp.take(blocks, spare_ids, axis=0).reshape(spare_rows, features)
    spare_weights = jnp.take(weights, spare_ids, axis=0)
    dom_count = lax.axis_size("dom")
    self_index = lax.axis_index("dom")
    tally = jnp.stack([jnp.sum(doubled), jnp.sum(discarded_rows)]).astype(jnp.float32)
    own_row = jnp.concatenate(
        [spare_weights.reshape(-1), tally, jnp.zeros((128 - block_rows - 2,), jnp.float32)]
    ).reshape(1, 128)
    all_rows = broadcast_rows(own_row, dom_count).reshape(dom_count, 128)
    tallies = all_rows[:, block_rows : block_rows + 2].astype(jnp.int32)
    before_mask = jnp.tril(jnp.ones((dom_count, dom_count), jnp.int32), -1)
    starts = jnp.sum(before_mask[:, :, None] * tallies[None], axis=1)
    wanted = (
        (tallies[:, 1] == 1)[:, None]
        & (tallies[:, 0] == 1)[None, :]
        & (starts[:, 1][:, None] == starts[:, 0][None, :])
    )
    held = lax.all_to_all(to_pieces(spare_blocks), "dom", 0, 0, tiled=True)
    piece_shape = held.shape
    routed = jnp.dot(
        wanted.astype(jnp.bfloat16),
        held.reshape(dom_count, -1),
        preferred_element_type=jnp.float32,
    ).astype(jnp.bfloat16)
    filled = from_pieces(lax.all_to_all(routed.reshape(piece_shape), "dom", 0, 0, tiled=True))
    own_wanted = lax.dynamic_slice_in_dim(wanted, self_index, 1)[0]
    filled_weights = jnp.sum(
        jnp.where(own_wanted[:, None], all_rows[:, :block_rows], 0.0), axis=0
    )
    vacant = discarded_rows == 1
    blocks = jnp.where(vacant[:, None, None], filled[None], blocks)
    weights = jnp.where(vacant[:, None], filled_weights[None], weights)
    groups = lax.axis_size("temp")
    even = [(i, i + 1 - 2 * (i % 2)) for i in range(groups)]
    odd = [(i, i - 1 + 2 * (i % 2)) for i in range(1, groups - 1)]
    blocks = neighbour_swap(blocks, even_pairs[0], even)
    blocks = neighbour_swap(blocks, odd_pairs[0], odd)
    row_data = blocks.reshape(block_count * block_rows, features)
    moved, log_det = transport(row_data, flow_in, flow_mid, flow_out)
    before = energy(row_data, energy_in, energy_mid, energy_out)
    after = energy(moved, energy_in, energy_mid, energy_out)
    updated = (
        weights.reshape(-1) + log_det - inverse_temp[0] * (new_level * after - old_level * before)
    )
    own_peak = jnp.max(updated)
    shifted = jnp.exp(updated - own_peak)
    own_stats = jnp.stack([own_peak, jnp.sum(shifted), jnp.sum(shifted * shifted)])
    own_stats = jnp.concatenate([own_stats, jnp.zeros((125,), jnp.float32)]).reshape(1, 128)
    stats = broadcast_rows(own_stats, dom_count).reshape(dom_count, 128)
    peak = jnp.max(stats[:, 0])
    factor = jnp.exp(stats[:, 0] - peak)
    first_sum = jnp.sum(stats[:, 1] * factor)
    second_sum = jnp.sum(stats[:, 2] * factor * factor)
    particle_total = updated.shape[0] * dom_count
    new_log_weights = updated - (peak + jnp.log(first_sum))
    log_ess = 2.0 * jnp.log(first_sum) - jnp.log(second_sum) - jnp.log(jnp.float32(particle_total))
    return (moved.reshape(1, -1, features), new_log_weights.reshape(1, -1), log_ess.reshape(1))


def solution(mesh):
    in_specs = (
        P("temp", "dom", None),
        P("temp", "dom"),
        P("temp", "dom"),
        P("temp", "dom"),
        P("temp", "dom"),
        P("temp"),
        P(),
        P(),
        P(),
        P(),
        P(),
        P(),
    )
    out_specs = (P("temp", "dom", None), P("temp", "dom"), P("temp"))
    return jax.shard_map(
        per_device, mesh=mesh, in_specs=in_specs, out_specs=out_specs, check_vma=False
    )
```

```python
import functools

import jax
import jax.numpy as jnp
from jax import lax
from jax.experimental import pallas as pl
from jax.experimental.pallas import tpu as pltpu
from jax.sharding import PartitionSpec as P

SWAPS = 2
TILE = 8
LANES = 128

old_level = 0.5
new_level = 0.75
scale_limit = 0.05

F32 = jnp.float32
BF16 = jnp.bfloat16
SMEM = pl.BlockSpec(memory_space=pltpu.SMEM)
VMEM = pl.BlockSpec(memory_space=pltpu.VMEM)
ANY = pl.BlockSpec(memory_space=pl.ANY)


def gelu(x):
    return x * (0.5 * (1.0 + jnp.tanh(0.7978845608028654 * (x + 0.044715 * (x * x * x)))))


def inside(x):
    return pltpu.with_memory_space_constraint(x, pltpu.VMEM)


def mul(a, b):
    return jnp.dot(a, b, preferred_element_type=F32)


def find(flags, value):
    slot = jnp.int32(-1)
    for b in range(flags.shape[1]):
        slot = jnp.where(flags[0, b] == value, b, slot)
    return slot


def find_two(flags):
    count = flags.shape[1]
    first, second = jnp.int32(count), jnp.int32(count)
    for b in reversed(range(count)):
        hit = flags[0, b] == 1
        second = jnp.where(hit, first, second)
        first = jnp.where(hit, b, first)
    return first, second


def spread(flags, width):
    count = flags.shape[1]
    slot = lax.broadcasted_iota(jnp.int32, (1, width), 1) // (width // count)
    row = jnp.zeros((1, width), jnp.int32)
    for b in range(count):
        row = jnp.where(slot == b, flags[0, b], row)
    return row


def step_rows(rows, weights, read_out, ready, keep, chunk):
    flow_in, flow_mid, flow_out, energy_in, energy_mid = weights
    half = rows.shape[1] // 2
    kept = rows[:, :half]
    ready(0)
    hidden = gelu(mul(kept, flow_in[...])).astype(BF16)
    ready(1)
    hidden = gelu(mul(hidden, flow_mid[...])).astype(BF16)
    ready(2)
    log_det = jnp.zeros((rows.shape[0], 1), F32)
    parts = []
    for at in range(0, half, chunk):
        log_scale = scale_limit * jnp.tanh(mul(hidden, flow_out[:, at : at + chunk]))
        shift = mul(hidden, flow_out[:, half + at : half + at + chunk])
        log_det += jnp.sum(log_scale, axis=1, keepdims=True)
        moved = rows[:, half + at : half + at + chunk].astype(F32)
        moved = (moved * jnp.exp(log_scale) + shift).astype(BF16)
        keep(half + at, moved)
        parts.append(moved)
    ready(3)
    base = mul(kept, energy_in[:half, :])
    before = base + mul(rows[:, half:], energy_in[half:, :])
    after = base + mul(jnp.concatenate(parts, axis=1), energy_in[half:, :])
    ready(4)
    levels = []
    for value in (before, after):
        unit = gelu(mul(gelu(value).astype(BF16), energy_mid[...]))
        levels.append(jnp.sum(unit * read_out, axis=1, keepdims=True))
    return log_det, new_level * levels[1] - old_level * levels[0]


def fetches(sources, targets, sems):
    return [
        pltpu.make_async_copy(source, target, sems.at[i])
        for i, (source, target) in enumerate(zip(sources, targets, strict=True))
    ]


def split(value, terms):
    parts = []
    for _ in range(terms):
        part = value.astype(BF16).astype(F32)
        parts.append(part)
        value = value - part
    return parts


def spare_kernel(
    counts, log_weights, read_out, particles, w0, w1, w2, w3, w4, out, rows, s0, s1, s2, s3, s4, sems, row_sem
):
    scratch = (s0, s1, s2, s3, s4)
    copies = fetches((w0, w1, w2, w3, w4), scratch, sems)
    block_rows = rows.shape[0]
    spare, vacant = find(counts, 2), find(counts, 0)
    slot = jnp.maximum(spare, 0)
    own = pltpu.make_async_copy(
        particles.at[pl.ds(pl.multiple_of(slot * block_rows, block_rows), block_rows), :], rows, row_sem
    )
    own.start()
    for copy in copies:
        copy.start()
    own.wait()
    width = rows.shape[1] // 4

    def keep(at, moved):
        done = 0
        while done < moved.shape[1]:
            c, start = divmod(at + done, width)
            size = min(moved.shape[1] - done, width - start)
            out[c * block_rows : (c + 1) * block_rows, start : start + size] = moved[:, done : done + size]
            done += size

    log_det, level = step_rows(
        rows, scratch, read_out[...], lambda i: copies[i].wait(), keep, width
    )
    for c in range(2):
        out[c * block_rows : (c + 1) * block_rows, :width] = rows[:, c * width : (c + 1) * width]
    lane = lax.broadcasted_iota(jnp.int32, (block_rows, LANES), 1)
    table = jnp.where(lane == 0, log_det, jnp.where(lane == 1, level, 0.0))
    table = jnp.concatenate([table] * (LANES // block_rows), axis=0).T
    weight = jnp.zeros((1, LANES), F32)
    for j in range(log_weights.shape[1] // LANES):
        weight = jnp.where(slot // 2 == j, log_weights[:, j * LANES : (j + 1) * LANES], weight)
    weight = jnp.where(slot % 2 == 0, weight, pltpu.roll(weight, LANES // 2, 1))
    weight = weight - jnp.log(jnp.full((1, LANES), 2.0, F32))
    terms = split(weight, 3) + split(table[0:1, :], 2) + split(table[1:2, :], 3)
    row = lax.broadcasted_iota(jnp.int32, (TILE, LANES), 0)
    lane = lax.broadcasted_iota(jnp.int32, (TILE, LANES), 1)
    extra = jnp.zeros((TILE, LANES), F32)
    for i, term in enumerate(terms):
        extra = jnp.where(row == i, term, extra)
    flag = jnp.where(lane < 96, (spare >= 0).astype(F32), (vacant >= 0).astype(F32))
    extra = jnp.where(lane < LANES // 2, extra, flag)
    out[:, width:] = jnp.concatenate([extra] * (out.shape[0] // TILE), axis=0).astype(BF16)


def rows_kernel(
    read_out, rows, w0, w1, w2, w3, w4, out, scalars, s0, s1, s2, s3, s4, sems
):
    scratch = (s0, s1, s2, s3, s4)
    copies = fetches((w0, w1, w2, w3, w4), scratch, sems)
    first = pl.program_id(0) == 0

    @pl.when(first)
    def _():
        for copy in copies:
            copy.start()

    def ready(i):
        @pl.when(first)
        def _():
            copies[i].wait()

    def keep(at, moved):
        out[:, at : at + moved.shape[1]] = moved

    half = rows.shape[1] // 2
    out[:, :half] = rows[:, :half]
    log_det, level = step_rows(rows, scratch, read_out[...], ready, keep, 512)
    lane = lax.broadcasted_iota(jnp.int32, (rows.shape[0], LANES), 1)
    table = jnp.where(lane == 0, log_det, jnp.where(lane == 1, level, 0.0)).T
    scalars[...] = table[:TILE, :]


def route_kernel(me, counts, log_weights, held, scalars, out, mine, tags):
    size = held.shape[0]
    width = out.shape[1]
    tag = held[:, width:]
    flags = tag.astype(F32)
    turned = flags.T
    half, late = LANES // 2, 96
    spare_col, vacant_col = flags[:, half : half + 1], flags[:, late : late + 1]
    spare_row, vacant_row = turned[half : half + 1, :], turned[late : late + 1, :]
    to = lax.broadcasted_iota(jnp.int32, (size, size), 0)
    source = lax.broadcasted_iota(jnp.int32, (size, size), 1)
    to_dev, source_dev = to // TILE, source // TILE
    vacant_rank = jnp.sum(jnp.where(source_dev < to_dev, vacant_row, 0.0), axis=1, keepdims=True)
    spare_rank = jnp.sum(jnp.where(to_dev < source_dev, spare_col, 0.0), axis=0, keepdims=True)
    hit = (vacant_rank == spare_rank) & (to % TILE == source % TILE)
    hit = hit & (vacant_col > 0.5) & (spare_row > 0.5)
    pick = jnp.where(hit, 1.0, 0.0).astype(BF16)
    out[...] = mul(pick, held[:, :width]).astype(BF16)
    tags[...] = mul(pick, tag)
    got = tags[pl.ds(pl.multiple_of(me[0] * TILE, TILE), TILE), :]
    total = log_weights.shape[1]

    def lay(value):
        lane = lax.broadcasted_iota(jnp.int32, (1, LANES), 1)
        value = jnp.where(lane < half, value, pltpu.roll(value, half, 1))
        return jnp.concatenate([value] * (total // LANES), axis=1)

    count = spread(counts, total)
    vacant = count == 0
    weight = log_weights[...] - jnp.log(jnp.maximum(count, 1).astype(F32))
    weight = jnp.where(vacant, lay(got[0:1] + got[1:2] + got[2:3]), weight)
    log_det = jnp.where(vacant, lay(got[3:4] + got[4:5]), scalars[0:1, :])
    level = jnp.where(vacant, lay(got[5:6] + got[6:7] + got[7:8]), scalars[1:2, :])
    row = lax.broadcasted_iota(jnp.int32, (TILE, total), 0)
    mine[...] = jnp.where(row == 0, log_det, jnp.where(row == 1, level, jnp.where(row == 2, weight, 0.0)))


def mix_kernel(flags, own, other, out):
    total = own.shape[1]
    take = spread(flags, total) == 1
    row = lax.broadcasted_iota(jnp.int32, own.shape, 0)
    out[...] = jnp.where(take & (row < 2), other[...], own[...])


def stats_kernel(flags, inverse_temp, own, other, updated, stats):
    take = spread(flags, own.shape[1]) == 1
    log_det = jnp.where(take, other[0:1, :], own[0:1, :])
    level = jnp.where(take, other[1:2, :], own[1:2, :])
    new = own[2:3, :] + log_det - inverse_temp[0] * level
    updated[...] = new
    peak = jnp.max(new, axis=1, keepdims=True)
    shifted = jnp.exp(new - peak)
    one = jnp.sum(shifted, axis=1, keepdims=True)
    two = jnp.sum(shifted * shifted, axis=1, keepdims=True)
    lane = lax.broadcasted_iota(jnp.int32, stats.shape, 1)
    stats[...] = jnp.where(lane == 0, peak, jnp.where(lane == 1, one, two))


def final_kernel(particle_total, updated, stats, new_weights, ess):
    table = stats[...]
    peaks = table[:, 0:1]
    peak = jnp.max(peaks, axis=0, keepdims=True)
    factor = jnp.exp(peaks - peak)
    one = jnp.sum(table[:, 1:2] * factor, axis=0, keepdims=True) * (1.0 / TILE)
    two = jnp.sum(table[:, 2:3] * factor * factor, axis=0, keepdims=True) * (1.0 / TILE)
    log_one = jnp.log(one)
    new_weights[...] = updated[...] - (peak + log_one)
    count = jnp.log(jnp.full((1, 1), particle_total, F32))
    ess[0] = jnp.max(2.0 * log_one - jnp.log(two) - count)


def at_slot(ref, slot, block_rows):
    return ref.at[pl.ds(pl.multiple_of(slot * block_rows, block_rows), block_rows), :]


def run(copies):
    for go, copy in copies:

        @pl.when(go)
        def _():
            copy.start()

    for go, copy in copies:

        @pl.when(go)
        def _():
            copy.wait()


def fill_kernel(counts, pairs, rows_in, pieces, later, rows, packed, sems):
    del rows_in, later
    block_rows = packed.shape[0] // SWAPS
    width = pieces.shape[1]
    slots = counts.shape[1]
    vacant = find(counts, 0)
    target = at_slot(rows, jnp.maximum(vacant, 0), block_rows)
    copies = []
    for c in range(4):
        source = pieces.at[c * block_rows : (c + 1) * block_rows, :]
        to = target.at[:, c * width : (c + 1) * width]
        copies.append((vacant >= 0, pltpu.make_async_copy(source, to, sems.at[c])))
    for i, slot in enumerate(find_two(pairs)):
        part = slice(i * block_rows, (i + 1) * block_rows)
        source = at_slot(rows, jnp.minimum(slot, slots - 1), block_rows)
        go = (slot < slots) & (slot != vacant)
        copies.append((go, pltpu.make_async_copy(source, packed.at[part, :], sems.at[4 + i])))

        @pl.when(slot == vacant)
        def _():
            for c in range(4):
                packed[part, c * width : (c + 1) * width] = pieces[c * block_rows : (c + 1) * block_rows, :]

    run(copies)


def swap_kernel(flags, next_flags, rows_in, received, rows, packed, sems):
    del rows_in
    block_rows = received.shape[0] // SWAPS
    slots = flags.shape[1]
    chosen = find_two(flags)
    parts = [slice(i * block_rows, (i + 1) * block_rows) for i in range(SWAPS)]
    copies = []
    for i, slot in enumerate(chosen):
        to = at_slot(rows, jnp.minimum(slot, slots - 1), block_rows)
        copies.append((slot < slots, pltpu.make_async_copy(received.at[parts[i], :], to, sems.at[i])))
    for i, slot in enumerate(find_two(next_flags)):
        source = at_slot(rows, jnp.minimum(slot, slots - 1), block_rows)
        go = (slot < slots) & (slot != chosen[0]) & (slot != chosen[1])
        copies.append((go, pltpu.make_async_copy(source, packed.at[parts[i], :], sems.at[SWAPS + i])))
        for j in range(SWAPS):

            @pl.when((slot < slots) & (slot == chosen[j]))
            def _():
                packed[parts[i], :] = received[parts[j], :]

    run(copies)


def last_kernel(flags, rows_in, received, rows, sems):
    del rows_in
    block_rows = received.shape[0] // SWAPS
    slots = flags.shape[1]
    copies = []
    for i, slot in enumerate(find_two(flags)):
        source = received.at[i * block_rows : (i + 1) * block_rows, :]
        to = at_slot(rows, jnp.minimum(slot, slots - 1), block_rows)
        copies.append((slot < slots, pltpu.make_async_copy(source, to, sems.at[i])))
    run(copies)


def per_device(
    particles,
    log_weights,
    offspring,
    even_pairs,
    odd_pairs,
    inverse_temp,
    flow_in,
    flow_mid,
    flow_out,
    energy_in,
    energy_mid,
    energy_out,
):
    block_count = offspring.shape[1]
    total, features = particles.shape[1:]
    block_rows = total // block_count
    hidden = flow_mid.shape[0]
    dom_count = lax.axis_size("dom")
    groups = lax.axis_size("temp")
    width = features // 4
    rows = particles.reshape(total, features)
    weights = (flow_in, flow_mid, flow_out, energy_in, energy_mid)
    read_out = energy_out.reshape(1, hidden)
    held_rows = dom_count * TILE
    weight_scratch = [pltpu.VMEM(w.shape, w.dtype) for w in weights]
    shape = jax.ShapeDtypeStruct
    weight_bytes = sum(2 * w.size for w in weights)

    def cost(count):
        flops = 2 * count * (sum(w.size for w in weights) + energy_in.size // 2)
        return pl.CostEstimate(
            flops=flops, transcendentals=count * features * 2, bytes_accessed=weight_bytes
        )

    pieces = pl.pallas_call(
        spare_kernel,
        out_shape=shape((held_rows, width + LANES), BF16),
        in_specs=[SMEM, VMEM, VMEM, ANY] + [ANY] * 5,
        out_specs=VMEM,
        scratch_shapes=[pltpu.VMEM((block_rows, features), BF16)]
        + weight_scratch
        + [pltpu.SemaphoreType.DMA((5,)), pltpu.SemaphoreType.DMA(())],
        cost_estimate=cost(block_rows),
        name="spare",
    )(offspring, log_weights, read_out, rows, *weights)

    def exchange(x):
        cut = x.reshape(dom_count, TILE, x.shape[1])
        return lax.all_to_all(cut, "dom", 0, 0, tiled=True).reshape(x.shape)

    held = exchange(pieces)
    step = total // 2
    done, scalars = pl.pallas_call(
        rows_kernel,
        out_shape=(shape((total, features), BF16), shape((TILE, total), F32)),
        grid=(2,),
        in_specs=[
            pl.BlockSpec((1, hidden), lambda i: (0, 0)),
            pl.BlockSpec((step, features), lambda i: (i, 0)),
        ]
        + [ANY] * 5,
        out_specs=(
            pl.BlockSpec((step, features), lambda i: (i, 0)),
            pl.BlockSpec((TILE, step), lambda i: (0, i)),
        ),
        scratch_shapes=weight_scratch + [pltpu.SemaphoreType.DMA((5,))],
        cost_estimate=cost(total),
        name="rows",
    )(read_out, rows, *weights)

    me = lax.axis_index("dom").astype(jnp.int32).reshape(1)
    routed, mine = pl.pallas_call(
        route_kernel,
        out_shape=(shape((held_rows, width), BF16), shape((TILE, total), F32)),
        in_specs=[SMEM, SMEM, VMEM, VMEM, VMEM],
        out_specs=(VMEM, VMEM),
        scratch_shapes=[pltpu.VMEM((held_rows, LANES), F32)],
        name="route",
    )(me, offspring, log_weights, inside(held), inside(scalars))
    filled = exchange(routed)

    even = [(i, i + 1 - 2 * (i % 2)) for i in range(groups)]
    odd = [(i, i - 1 + 2 * (i % 2)) for i in range(1, groups - 1)]
    other = lax.ppermute(mine, "temp", even)
    mixed = pl.pallas_call(
        mix_kernel,
        out_shape=shape((TILE, total), F32),
        in_specs=[SMEM, VMEM, VMEM],
        out_specs=VMEM,
        name="mix",
    )(even_pairs, mine, inside(other))
    other = lax.ppermute(mixed, "temp", odd)
    updated, stats = pl.pallas_call(
        stats_kernel,
        out_shape=(shape((1, total), F32), shape((held_rows, LANES), F32)),
        in_specs=[SMEM, SMEM, VMEM, VMEM],
        out_specs=(VMEM, VMEM),
        name="stats",
    )(odd_pairs, inverse_temp, mixed, inside(other))
    stats = exchange(stats)
    new_log_weights, log_ess = pl.pallas_call(
        functools.partial(final_kernel, float(total * dom_count)),
        out_shape=(shape((1, total), F32), shape((1,), F32)),
        in_specs=[VMEM, VMEM],
        out_specs=(VMEM, SMEM),
        name="final",
    )(updated, inside(stats))

    whole = shape((total, features), BF16)
    pack = shape((SWAPS * block_rows, features), BF16)
    done, packed = pl.pallas_call(
        fill_kernel,
        out_shape=(whole, pack),
        in_specs=[SMEM, SMEM, ANY, VMEM, ANY],
        out_specs=(ANY, VMEM),
        scratch_shapes=[pltpu.SemaphoreType.DMA((4 + SWAPS,))],
        input_output_aliases={2: 0},
        name="fill",
    )(offspring, even_pairs, done, inside(filled), updated)
    received = lax.ppermute(packed, "temp", even)
    done, packed = pl.pallas_call(
        swap_kernel,
        out_shape=(whole, pack),
        in_specs=[SMEM, SMEM, ANY, VMEM],
        out_specs=(ANY, VMEM),
        scratch_shapes=[pltpu.SemaphoreType.DMA((2 * SWAPS,))],
        input_output_aliases={2: 0},
        name="even",
    )(even_pairs, odd_pairs, done, inside(received))
    received = lax.ppermute(packed, "temp", odd)
    done = pl.pallas_call(
        last_kernel,
        out_shape=whole,
        in_specs=[SMEM, ANY, VMEM],
        out_specs=ANY,
        scratch_shapes=[pltpu.SemaphoreType.DMA((SWAPS,))],
        input_output_aliases={1: 0},
        name="odd",
    )(odd_pairs, done, inside(received))
    return done.reshape(1, total, features), new_log_weights, log_ess


def solution(mesh):
    in_specs = (
        P("temp", "dom", None),
        P("temp", "dom"),
        P("temp", "dom"),
        P("temp", "dom"),
        P("temp", "dom"),
        P("temp"),
        P(),
        P(),
        P(),
        P(),
        P(),
        P(),
    )
    out_specs = (P("temp", "dom", None), P("temp", "dom"), P("temp"))
    return jax.shard_map(
        per_device, mesh=mesh, in_specs=in_specs, out_specs=out_specs, check_vma=False
    )
```

```python
import functools

import jax
import jax.numpy as jnp
from jax import lax
from jax.experimental import pallas as pl
from jax.experimental.pallas import tpu as pltpu
from jax.sharding import PartitionSpec as P


SWAPS = 2
TILE = 8
LANES = 128

old_level = 0.5
new_level = 0.75
scale_limit = 0.05

F32 = jnp.float32
BF16 = jnp.bfloat16
SMEM = pl.BlockSpec(memory_space=pltpu.SMEM)
VMEM = pl.BlockSpec(memory_space=pltpu.VMEM)
ANY = pl.BlockSpec(memory_space=pl.ANY)


def gelu(x):
    half = 0.5 * x
    inner = x * (0.7978845608028654 + (0.7978845608028654 * 0.044715) * (x * x))
    return half + half * jnp.tanh(inner)


def inside(x):
    return pltpu.with_memory_space_constraint(x, pltpu.VMEM)


def mul(a, b):
    return jnp.dot(a, b, preferred_element_type=F32)


def find(flags, value):
    slot = jnp.int32(-1)
    for b in range(flags.shape[1]):
        slot = jnp.where(flags[0, b] == value, b, slot)
    return slot


def find_two(flags):
    count = flags.shape[1]
    first, second = jnp.int32(count), jnp.int32(count)
    for b in reversed(range(count)):
        hit = flags[0, b] == 1
        second = jnp.where(hit, first, second)
        first = jnp.where(hit, b, first)
    return first, second


def spread(flags, width):
    count = flags.shape[1]
    slot = lax.broadcasted_iota(jnp.int32, (1, width), 1) // (width // count)
    row = jnp.zeros((1, width), jnp.int32)
    for b in range(count):
        row = jnp.where(slot == b, flags[0, b], row)
    return row


def step_rows(rows, weights, read_out, ready, keep, chunk):
    flow_in, flow_mid, flow_out, energy_in, energy_mid = weights
    half = rows.shape[1] // 2
    kept = rows[:, :half]
    ready(0)
    hidden = gelu(mul(kept, flow_in[...])).astype(BF16)
    ready(1)
    hidden = gelu(mul(hidden, flow_mid[...])).astype(BF16)
    ready(2)
    log_det = jnp.zeros((rows.shape[0], 1), F32)
    parts, olds = [], []
    for at in range(0, half, chunk):
        log_scale = scale_limit * jnp.tanh(mul(hidden, flow_out[:, at : at + chunk]))
        shift = mul(hidden, flow_out[:, half + at : half + at + chunk])
        log_det += jnp.sum(log_scale, axis=1, keepdims=True)
        old = rows[:, half + at : half + at + chunk]
        moved = (old.astype(F32) * jnp.exp(log_scale) + shift).astype(BF16)
        keep(half + at, moved)
        parts.append(moved)
        olds.append(old)
    ready(3)
    base = mul(kept, energy_in[:half, :])
    before = base + mul(jnp.concatenate(olds, axis=1), energy_in[half:, :])
    after = base + mul(jnp.concatenate(parts, axis=1), energy_in[half:, :])
    ready(4)
    levels = []
    for value in (before, after):
        unit = gelu(mul(gelu(value).astype(BF16), energy_mid[...]))
        levels.append(jnp.sum(unit * read_out, axis=1, keepdims=True))
    return log_det, new_level * levels[1] - old_level * levels[0]


def fetches(sources, targets, sems):
    return [
        pltpu.make_async_copy(source, target, sems.at[i])
        for i, (source, target) in enumerate(zip(sources, targets, strict=True))
    ]


def split(value, terms):
    parts = []
    for _ in range(terms):
        part = value.astype(BF16).astype(F32)
        parts.append(part)
        value = value - part
    return parts


def spare_kernel(
    counts, log_weights, read_out, particles, w0, w1, w2, w3, w4, out, rows, s0, s1, s2, s3, s4, sems, row_sem
):
    scratch = (s0, s1, s2, s3, s4)
    copies = fetches((w0, w1, w2, w3, w4), scratch, sems)
    block_rows = rows.shape[0]
    spare, vacant = find(counts, 2), find(counts, 0)
    slot = jnp.maximum(spare, 0)
    own = pltpu.make_async_copy(
        particles.at[pl.ds(pl.multiple_of(slot * block_rows, block_rows), block_rows), :], rows, row_sem
    )
    own.start()
    for copy in copies:
        copy.start()
    own.wait()
    width = rows.shape[1] // 4

    def keep(at, moved):
        done = 0
        while done < moved.shape[1]:
            c, start = divmod(at + done, width)
            size = min(moved.shape[1] - done, width - start)
            out[c * block_rows : (c + 1) * block_rows, start : start + size] = moved[:, done : done + size]
            done += size

    log_det, level = step_rows(
        rows, scratch, read_out[...], lambda i: copies[i].wait(), keep, width
    )
    for c in range(2):
        out[c * block_rows : (c + 1) * block_rows, :width] = rows[:, c * width : (c + 1) * width]
    lane = lax.broadcasted_iota(jnp.int32, (block_rows, LANES), 1)
    table = jnp.where(lane == 0, log_det, jnp.where(lane == 1, level, 0.0))
    table = jnp.concatenate([table] * (LANES // block_rows), axis=0).T
    weight = jnp.zeros((1, LANES), F32)
    for j in range(log_weights.shape[1] // LANES):
        weight = jnp.where(slot // 2 == j, log_weights[:, j * LANES : (j + 1) * LANES], weight)
    weight = jnp.where(slot % 2 == 0, weight, pltpu.roll(weight, LANES // 2, 1))
    weight = weight - jnp.log(jnp.full((1, LANES), 2.0, F32))
    terms = split(weight, 3) + split(table[0:1, :], 2) + split(table[1:2, :], 3)
    row = lax.broadcasted_iota(jnp.int32, (TILE, LANES), 0)
    lane = lax.broadcasted_iota(jnp.int32, (TILE, LANES), 1)
    extra = jnp.zeros((TILE, LANES), F32)
    for i, term in enumerate(terms):
        extra = jnp.where(row == i, term, extra)
    flag = jnp.where(lane < 96, (spare >= 0).astype(F32), (vacant >= 0).astype(F32))
    extra = jnp.where(lane < LANES // 2, extra, flag)
    out[:, width:] = jnp.concatenate([extra] * (out.shape[0] // TILE), axis=0).astype(BF16)


def rows_kernel(
    pairs, read_out, particles, w0, w1, w2, w3, w4, out, scalars, packed, s0, s1, s2, s3, s4, rows, sems, row_sem, out_sem
):
    scratch = (s0, s1, s2, s3, s4)
    copies = fetches((w0, w1, w2, w3, w4), scratch, sems)
    half = rows.shape[1] // 2
    parts = [slice(0, half), slice(half, 2 * half)]
    loads = [pltpu.make_async_copy(particles.at[:, p], rows.at[:, p], row_sem.at[i]) for i, p in enumerate(parts)]
    loads[0].start()
    copies[0].start()
    copies[1].start()
    copies[2].start()
    loads[1].start()
    copies[3].start()
    copies[4].start()

    def ready(i):
        copies[i].wait()
        if i == 2:
            loads[1].wait()

    loads[0].wait()
    kept_out = pltpu.make_async_copy(rows.at[:, parts[0]], out.at[:, parts[0]], out_sem.at[0])
    kept_out.start()

    def keep(at, moved):
        rows[:, at : at + moved.shape[1]] = moved

    log_det, level = step_rows(rows, scratch, read_out[...], ready, keep, 512)
    moved_out = pltpu.make_async_copy(rows.at[:, parts[1]], out.at[:, parts[1]], out_sem.at[1])
    moved_out.start()
    lane = lax.broadcasted_iota(jnp.int32, (rows.shape[0], LANES), 1)
    table = jnp.where(lane == 0, log_det, jnp.where(lane == 1, level, 0.0)).T
    scalars[...] = table[:TILE, :]
    block_rows = packed.shape[0] // SWAPS
    slots = pairs.shape[1]
    for i, slot in enumerate(find_two(pairs)):
        start = pl.multiple_of(jnp.minimum(slot, slots - 1) * block_rows, block_rows)
        packed[i * block_rows : (i + 1) * block_rows, :] = rows[pl.ds(start, block_rows), :]
    kept_out.wait()
    moved_out.wait()


def route_kernel(me, counts, pairs, log_weights, held, scalars, out, mine, tags):
    size = held.shape[0]
    width = out.shape[1]
    tag = held[:, width:]
    flags = tag.astype(F32)
    turned = flags.T
    half, late = LANES // 2, 96
    spare_col, vacant_col = flags[:, half : half + 1], flags[:, late : late + 1]
    spare_row, vacant_row = turned[half : half + 1, :], turned[late : late + 1, :]
    to = lax.broadcasted_iota(jnp.int32, (size, size), 0)
    source = lax.broadcasted_iota(jnp.int32, (size, size), 1)
    to_dev, source_dev = to // TILE, source // TILE
    vacant_rank = jnp.sum(jnp.where(source_dev < to_dev, vacant_row, 0.0), axis=1, keepdims=True)
    spare_rank = jnp.sum(jnp.where(to_dev < source_dev, spare_col, 0.0), axis=0, keepdims=True)
    hit = (vacant_rank == spare_rank) & (to % TILE == source % TILE)
    hit = hit & (vacant_col > 0.5) & (spare_row > 0.5)
    pick = jnp.where(hit, 1.0, 0.0).astype(BF16)
    out[...] = mul(pick, held[:, :width]).astype(BF16)
    tags[...] = mul(pick, tag)
    got = tags[pl.ds(pl.multiple_of(me[0] * TILE, TILE), TILE), :]
    total = log_weights.shape[1]

    def lay(value):
        lane = lax.broadcasted_iota(jnp.int32, (1, LANES), 1)
        value = jnp.where(lane < half, value, pltpu.roll(value, half, 1))
        return jnp.concatenate([value] * (total // LANES), axis=1)

    count = spread(counts, total)
    vacant = count == 0
    weight = log_weights[...] - jnp.log(jnp.maximum(count, 1).astype(F32))
    weight = jnp.where(vacant, lay(got[0:1] + got[1:2] + got[2:3]), weight)
    log_det = jnp.where(vacant, lay(got[3:4] + got[4:5]), scalars[0:1, :])
    level = jnp.where(vacant, lay(got[5:6] + got[6:7] + got[7:8]), scalars[1:2, :])
    row = lax.broadcasted_iota(jnp.int32, (TILE, total), 0)
    table = jnp.where(row == 0, log_det, jnp.where(row == 1, level, weight))
    mine[...] = jnp.where(row == 3, spread(pairs, total).astype(F32), table)


def stats_kernel(even, odd, inverse_temp, own, from_even, from_odd, from_both, updated, stats):
    total = own.shape[1]
    take_even, take_odd = spread(even, total) == 1, spread(odd, total) == 1
    beyond = from_odd[3:4, :] > 0.5

    def settle(r):
        line = slice(r, r + 1)
        swapped = jnp.where(take_even, from_even[line, :], own[line, :])
        return jnp.where(take_odd, jnp.where(beyond, from_both[line, :], from_odd[line, :]), swapped)

    new = own[2:3, :] + settle(0) - inverse_temp[0] * settle(1)
    updated[...] = new
    peak = jnp.max(new, axis=1, keepdims=True)
    shifted = jnp.exp(new - peak)
    one = jnp.sum(shifted, axis=1, keepdims=True)
    two = jnp.sum(shifted * shifted, axis=1, keepdims=True)
    lane = lax.broadcasted_iota(jnp.int32, stats.shape, 1)
    stats[...] = jnp.where(lane == 0, peak, jnp.where(lane == 1, one, two))


def final_kernel(particle_total, updated, stats, new_weights, ess):
    table = stats[...]
    peaks = table[:, 0:1]
    peak = jnp.max(peaks, axis=0, keepdims=True)
    factor = jnp.exp(peaks - peak)
    one = jnp.sum(table[:, 1:2] * factor, axis=0, keepdims=True) * (1.0 / TILE)
    two = jnp.sum(table[:, 2:3] * factor * factor, axis=0, keepdims=True) * (1.0 / TILE)
    log_one = jnp.log(one)
    new_weights[...] = updated[...] - (peak + log_one)
    count = jnp.log(jnp.full((1, 1), particle_total, F32))
    ess[0] = jnp.max(2.0 * log_one - jnp.log(two) - count)


def at_slot(ref, slot, block_rows):
    return ref.at[pl.ds(pl.multiple_of(slot * block_rows, block_rows), block_rows), :]


def join_kernel(
    counts, other_counts, even, odd, rows_in, filled, filled_other, received, later, rows, packed, sems
):
    del rows_in, later
    block_rows = packed.shape[0] // SWAPS
    width = filled.shape[1]
    slots = counts.shape[1]
    vacant, other_vacant = find(counts, 0), find(other_counts, 0)
    pair, odd_pair = find_two(even), find_two(odd)
    parts = [slice(i * block_rows, (i + 1) * block_rows) for i in range(SWAPS)]
    copies = []

    def spill(go, source, slot, sem):
        to = at_slot(rows, jnp.clip(slot, 0, slots - 1), block_rows)
        for c in range(4):
            part = source.at[c * block_rows : (c + 1) * block_rows, :]
            column = to.at[:, c * width : (c + 1) * width]
            copies.append((go, pltpu.make_async_copy(part, column, sems.at[sem + c])))

    def hold(go, source, i):
        @pl.when(go)
        def _():
            for c in range(4):
                packed[parts[i], c * width : (c + 1) * width] = source[c * block_rows : (c + 1) * block_rows, :]

    spill((vacant >= 0) & (vacant != pair[0]) & (vacant != pair[1]), filled, vacant, 0)
    spill((other_vacant >= 0) & ((other_vacant == pair[0]) | (other_vacant == pair[1])), filled_other, other_vacant, 4)
    for i, slot in enumerate(pair):
        to = at_slot(rows, jnp.minimum(slot, slots - 1), block_rows)
        go = (slot < slots) & (slot != other_vacant)
        copies.append((go, pltpu.make_async_copy(received.at[parts[i], :], to, sems.at[8 + i])))
    for i, slot in enumerate(odd_pair):
        swapped = (slot == pair[0]) | (slot == pair[1])
        source = at_slot(rows, jnp.minimum(slot, slots - 1), block_rows)
        go = (slot < slots) & (slot != vacant) & jnp.logical_not(swapped)
        copies.append((go, pltpu.make_async_copy(source, packed.at[parts[i], :], sems.at[8 + SWAPS + i])))
    for go, copy in copies:

        @pl.when(go)
        def _():
            copy.start()

    for i, slot in enumerate(odd_pair):
        swapped = (slot == pair[0]) | (slot == pair[1])
        hold((slot == vacant) & jnp.logical_not(swapped), filled, i)
        hold((slot < slots) & swapped & (slot == other_vacant), filled_other, i)
        for j in range(SWAPS):

            @pl.when((slot < slots) & (slot == pair[j]) & (slot != other_vacant))
            def _():
                packed[parts[i], :] = received[parts[j], :]

    for go, copy in copies:

        @pl.when(go)
        def _():
            copy.wait()


def last_kernel(flags, rows_in, received, rows, sems):
    del rows_in
    block_rows = received.shape[0] // SWAPS
    slots = flags.shape[1]
    copies = []
    for i, slot in enumerate(find_two(flags)):
        source = received.at[i * block_rows : (i + 1) * block_rows, :]
        to = at_slot(rows, jnp.minimum(slot, slots - 1), block_rows)
        copies.append((slot < slots, pltpu.make_async_copy(source, to, sems.at[i])))
    for go, copy in copies:

        @pl.when(go)
        def _():
            copy.start()

    for go, copy in copies:

        @pl.when(go)
        def _():
            copy.wait()


def per_device(
    particles,
    log_weights,
    offspring,
    even_pairs,
    odd_pairs,
    inverse_temp,
    flow_in,
    flow_mid,
    flow_out,
    energy_in,
    energy_mid,
    energy_out,
):
    block_count = offspring.shape[1]
    total, features = particles.shape[1:]
    block_rows = total // block_count
    hidden = flow_mid.shape[0]
    dom_count = lax.axis_size("dom")
    groups = lax.axis_size("temp")
    width = features // 4
    rows = particles.reshape(total, features)
    weights = (flow_in, flow_mid, flow_out, energy_in, energy_mid)
    read_out = energy_out.reshape(1, hidden)
    held_rows = dom_count * TILE
    weight_scratch = [pltpu.VMEM(w.shape, w.dtype) for w in weights]
    shape = jax.ShapeDtypeStruct
    weight_bytes = sum(2 * w.size for w in weights)

    def cost(count):
        flops = 2 * count * (sum(w.size for w in weights) + energy_in.size // 2)
        return pl.CostEstimate(
            flops=flops, transcendentals=count * features * 2, bytes_accessed=weight_bytes
        )

    pieces = pl.pallas_call(
        spare_kernel,
        out_shape=shape((held_rows, width + LANES), BF16),
        in_specs=[SMEM, VMEM, VMEM, ANY] + [ANY] * 5,
        out_specs=VMEM,
        scratch_shapes=[pltpu.VMEM((block_rows, features), BF16)]
        + weight_scratch
        + [pltpu.SemaphoreType.DMA((5,)), pltpu.SemaphoreType.DMA(())],
        cost_estimate=cost(block_rows),
        name="spare",
    )(offspring, log_weights, read_out, rows, *weights)

    def exchange(x):
        cut = x.reshape(dom_count, TILE, x.shape[1])
        cut = lax.all_to_all(cut, "dom", 0, 0, tiled=True)
        return cut.reshape(x.shape)

    def swap(x, pairs):
        return lax.ppermute(x, "temp", pairs)

    held = exchange(pieces)
    pack = shape((SWAPS * block_rows, features), BF16)
    done, scalars, packed = pl.pallas_call(
        rows_kernel,
        out_shape=(shape((total, features), BF16), shape((TILE, total), F32), pack),
        in_specs=[SMEM, VMEM, ANY] + [ANY] * 5,
        out_specs=(ANY, VMEM, VMEM),
        scratch_shapes=weight_scratch
        + [
            pltpu.VMEM((total, features), BF16),
            pltpu.SemaphoreType.DMA((5,)),
            pltpu.SemaphoreType.DMA((2,)),
            pltpu.SemaphoreType.DMA((2,)),
        ],
        cost_estimate=cost(total),
        name="rows",
    )(even_pairs, read_out, rows, *weights)
    even = [(i, i + 1 - 2 * (i % 2)) for i in range(groups)]
    odd = [(i, i - 1 + 2 * (i % 2)) for i in range(1, groups - 1)]
    both = [(even[source][1], target) for source, target in odd]
    received = swap(packed, even)
    other_counts = swap(offspring, even)

    me = lax.axis_index("dom").astype(jnp.int32).reshape(1)
    routed, mine = pl.pallas_call(
        route_kernel,
        out_shape=(shape((held_rows, width), BF16), shape((TILE, total), F32)),
        in_specs=[SMEM, SMEM, SMEM, VMEM, VMEM, VMEM],
        out_specs=(VMEM, VMEM),
        scratch_shapes=[pltpu.VMEM((held_rows, LANES), F32)],
        name="route",
    )(me, offspring, even_pairs, log_weights, inside(held), scalars)
    filled = exchange(routed)

    from_even = swap(mine, even)
    from_odd = swap(mine, odd)
    from_both = swap(mine, both)
    settle = pl.pallas_call(
        stats_kernel,
        out_shape=(shape((1, total), F32), shape((held_rows, LANES), F32)),
        in_specs=[SMEM, SMEM, SMEM, VMEM, VMEM, VMEM, VMEM],
        out_specs=(VMEM, VMEM),
        name="stats",
    )
    lines = [inside(line) for line in (from_even, from_odd, from_both)]
    updated, stats = settle(even_pairs, odd_pairs, inverse_temp, mine, *lines)
    stats = exchange(stats)
    close = pl.pallas_call(
        functools.partial(final_kernel, float(total * dom_count)),
        out_shape=(shape((1, total), F32), shape((1,), F32)),
        in_specs=[VMEM, VMEM],
        out_specs=(VMEM, SMEM),
        name="final",
    )
    new_log_weights, log_ess = close(updated, inside(stats))

    whole = shape((total, features), BF16)
    filled_other = swap(filled, even)
    done, packed = pl.pallas_call(
        join_kernel,
        out_shape=(whole, pack),
        in_specs=[SMEM] * 4 + [ANY] + [VMEM] * 3 + [ANY],
        out_specs=(ANY, VMEM),
        scratch_shapes=[pltpu.SemaphoreType.DMA((8 + 2 * SWAPS,))],
        input_output_aliases={4: 0},
        name="join",
    )(
        offspring,
        other_counts,
        even_pairs,
        odd_pairs,
        done,
        inside(filled),
        inside(filled_other),
        inside(received),
        updated,
    )
    received = swap(packed, odd)
    done = pl.pallas_call(
        last_kernel,
        out_shape=whole,
        in_specs=[SMEM, ANY, VMEM],
        out_specs=ANY,
        scratch_shapes=[pltpu.SemaphoreType.DMA((SWAPS,))],
        input_output_aliases={1: 0},
        name="odd",
    )(odd_pairs, done, inside(received))
    return done.reshape(1, total, features), new_log_weights, log_ess


def solution(mesh):
    in_specs = (
        P("temp", "dom", None),
        P("temp", "dom"),
        P("temp", "dom"),
        P("temp", "dom"),
        P("temp", "dom"),
        P("temp"),
        P(),
        P(),
        P(),
        P(),
        P(),
        P(),
    )
    out_specs = (P("temp", "dom", None), P("temp", "dom"), P("temp"))

    return jax.shard_map(per_device, mesh=mesh, in_specs=in_specs, out_specs=out_specs, check_vma=False)
```

```python
import functools

import jax
import jax.numpy as jnp
from jax import lax
from jax.experimental import pallas as pl
from jax.experimental.pallas import tpu as pltpu
from jax.sharding import PartitionSpec as P


SWAPS = 2
TILE = 8
LANES = 128

old_level = 0.5
new_level = 0.75
scale_limit = 0.05

F32 = jnp.float32
BF16 = jnp.bfloat16
SMEM = pl.BlockSpec(memory_space=pltpu.SMEM)
VMEM = pl.BlockSpec(memory_space=pltpu.VMEM)
ANY = pl.BlockSpec(memory_space=pl.ANY)


def gelu(x):
    half = 0.5 * x
    inner = x * (0.7978845608028654 + (0.7978845608028654 * 0.044715) * (x * x))
    return half + half * jnp.tanh(inner)


def inside(x):
    return pltpu.with_memory_space_constraint(x, pltpu.VMEM)


def mul(a, b):
    return jnp.dot(a, b, preferred_element_type=F32)


def find(flags, value):
    slot = jnp.int32(-1)
    for b in range(flags.shape[1]):
        slot = jnp.where(flags[0, b] == value, b, slot)
    return slot


def find_two(flags):
    count = flags.shape[1]
    first, second = jnp.int32(count), jnp.int32(count)
    for b in reversed(range(count)):
        hit = flags[0, b] == 1
        second = jnp.where(hit, first, second)
        first = jnp.where(hit, b, first)
    return first, second


def spread(flags, width):
    count = flags.shape[1]
    slot = lax.broadcasted_iota(jnp.int32, (1, width), 1) // (width // count)
    row = jnp.zeros((1, width), jnp.int32)
    for b in range(count):
        row = jnp.where(slot == b, flags[0, b], row)
    return row


def step_rows(rows, weights, read_out, ready, keep, chunk):
    flow_in, flow_mid, flow_out, energy_in, energy_mid = weights
    half = rows.shape[1] // 2
    kept = rows[:, :half]
    ready(0)
    hidden = gelu(mul(kept, flow_in[...])).astype(BF16)
    ready(1)
    hidden = gelu(mul(hidden, flow_mid[...])).astype(BF16)
    ready(2)
    log_det = jnp.zeros((rows.shape[0], 1), F32)
    parts, olds = [], []
    for at in range(0, half, chunk):
        log_scale = scale_limit * jnp.tanh(mul(hidden, flow_out[:, at : at + chunk]))
        shift = mul(hidden, flow_out[:, half + at : half + at + chunk])
        log_det += jnp.sum(log_scale, axis=1, keepdims=True)
        old = rows[:, half + at : half + at + chunk]
        moved = (old.astype(F32) * jnp.exp(log_scale) + shift).astype(BF16)
        keep(half + at, moved)
        parts.append(moved)
        olds.append(old)
    ready(3)
    base = mul(kept, energy_in[:half, :])
    before = base + mul(jnp.concatenate(olds, axis=1), energy_in[half:, :])
    after = base + mul(jnp.concatenate(parts, axis=1), energy_in[half:, :])
    ready(4)
    levels = []
    for value in (before, after):
        unit = gelu(mul(gelu(value).astype(BF16), energy_mid[...]))
        levels.append(jnp.sum(unit * read_out, axis=1, keepdims=True))
    return log_det, new_level * levels[1] - old_level * levels[0]


def fetches(sources, targets, sems):
    return [
        pltpu.make_async_copy(source, target, sems.at[i])
        for i, (source, target) in enumerate(zip(sources, targets, strict=True))
    ]


def split(value, terms):
    parts = []
    for _ in range(terms):
        part = value.astype(BF16).astype(F32)
        parts.append(part)
        value = value - part
    return parts


def spare_kernel(
    counts, log_weights, read_out, particles, w0, w1, w2, w3, w4, out, rows, s0, s1, s2, s3, s4, sems, row_sem
):
    scratch = (s0, s1, s2, s3, s4)
    copies = fetches((w0, w1, w2, w3, w4), scratch, sems)
    block_rows = rows.shape[0]
    spare, vacant = find(counts, 2), find(counts, 0)
    slot = jnp.maximum(spare, 0)
    own = pltpu.make_async_copy(
        particles.at[pl.ds(pl.multiple_of(slot * block_rows, block_rows), block_rows), :], rows, row_sem
    )
    own.start()
    for copy in copies:
        copy.start()
    own.wait()
    width = rows.shape[1] // 4

    def keep(at, moved):
        done = 0
        while done < moved.shape[1]:
            c, start = divmod(at + done, width)
            size = min(moved.shape[1] - done, width - start)
            out[c * block_rows : (c + 1) * block_rows, start : start + size] = moved[:, done : done + size]
            done += size

    log_det, level = step_rows(
        rows, scratch, read_out[...], lambda i: copies[i].wait(), keep, width
    )
    for c in range(2):
        out[c * block_rows : (c + 1) * block_rows, :width] = rows[:, c * width : (c + 1) * width]
    lane = lax.broadcasted_iota(jnp.int32, (block_rows, LANES), 1)
    table = jnp.where(lane == 0, log_det, jnp.where(lane == 1, level, 0.0))
    table = jnp.concatenate([table] * (LANES // block_rows), axis=0).T
    weight = jnp.zeros((1, LANES), F32)
    for j in range(log_weights.shape[1] // LANES):
        weight = jnp.where(slot // 2 == j, log_weights[:, j * LANES : (j + 1) * LANES], weight)
    weight = jnp.where(slot % 2 == 0, weight, pltpu.roll(weight, LANES // 2, 1))
    weight = weight - jnp.log(jnp.full((1, LANES), 2.0, F32))
    terms = split(weight, 3) + split(table[0:1, :], 2) + split(table[1:2, :], 3)
    row = lax.broadcasted_iota(jnp.int32, (TILE, LANES), 0)
    lane = lax.broadcasted_iota(jnp.int32, (TILE, LANES), 1)
    extra = jnp.zeros((TILE, LANES), F32)
    for i, term in enumerate(terms):
        extra = jnp.where(row == i, term, extra)
    flag = jnp.where(lane < 96, (spare >= 0).astype(F32), (vacant >= 0).astype(F32))
    extra = jnp.where(lane < LANES // 2, extra, flag)
    out[:, width:] = jnp.concatenate([extra] * (out.shape[0] // TILE), axis=0).astype(BF16)


def rows_kernel(
    pairs, read_out, particles, w0, w1, w2, w3, w4, out, scalars, packed, s0, s1, s2, s3, s4, rows, sems, row_sem, out_sem
):
    scratch = (s0, s1, s2, s3, s4)
    copies = fetches((w0, w1, w2, w3, w4), scratch, sems)
    half = rows.shape[1] // 2
    parts = [slice(0, half), slice(half, 2 * half)]
    loads = [pltpu.make_async_copy(particles.at[:, p], rows.at[:, p], row_sem.at[i]) for i, p in enumerate(parts)]
    loads[0].start()
    copies[0].start()
    copies[1].start()
    copies[2].start()
    loads[1].start()
    copies[3].start()
    copies[4].start()

    def ready(i):
        copies[i].wait()
        if i == 2:
            loads[1].wait()

    loads[0].wait()
    kept_out = pltpu.make_async_copy(rows.at[:, parts[0]], out.at[:, parts[0]], out_sem.at[0])
    kept_out.start()

    def keep(at, moved):
        rows[:, at : at + moved.shape[1]] = moved

    log_det, level = step_rows(rows, scratch, read_out[...], ready, keep, 512)
    moved_out = pltpu.make_async_copy(rows.at[:, parts[1]], out.at[:, parts[1]], out_sem.at[1])
    moved_out.start()
    lane = lax.broadcasted_iota(jnp.int32, (rows.shape[0], LANES), 1)
    table = jnp.where(lane == 0, log_det, jnp.where(lane == 1, level, 0.0)).T
    scalars[...] = table[:TILE, :]
    block_rows = packed.shape[0] // SWAPS
    slots = pairs.shape[1]
    for i, slot in enumerate(find_two(pairs)):
        start = pl.multiple_of(jnp.minimum(slot, slots - 1) * block_rows, block_rows)
        packed[i * block_rows : (i + 1) * block_rows, :] = rows[pl.ds(start, block_rows), :]
    kept_out.wait()
    moved_out.wait()


def route_kernel(me, counts, pairs, log_weights, held, scalars, out, mine, tags):
    size = held.shape[0]
    width = out.shape[1]
    tag = held[:, width:]
    flags = tag.astype(F32)
    turned = flags.T
    half, late = LANES // 2, 96
    spare_col, vacant_col = flags[:, half : half + 1], flags[:, late : late + 1]
    spare_row, vacant_row = turned[half : half + 1, :], turned[late : late + 1, :]
    to = lax.broadcasted_iota(jnp.int32, (size, size), 0)
    source = lax.broadcasted_iota(jnp.int32, (size, size), 1)
    to_dev, source_dev = to // TILE, source // TILE
    vacant_rank = jnp.sum(jnp.where(source_dev < to_dev, vacant_row, 0.0), axis=1, keepdims=True)
    spare_rank = jnp.sum(jnp.where(to_dev < source_dev, spare_col, 0.0), axis=0, keepdims=True)
    hit = (vacant_rank == spare_rank) & (to % TILE == source % TILE)
    hit = hit & (vacant_col > 0.5) & (spare_row > 0.5)
    pick = jnp.where(hit, 1.0, 0.0).astype(BF16)
    out[...] = mul(pick, held[:, :width]).astype(BF16)
    tags[...] = mul(pick, tag)
    got = tags[pl.ds(pl.multiple_of(me[0] * TILE, TILE), TILE), :]
    total = log_weights.shape[1]

    def lay(value):
        lane = lax.broadcasted_iota(jnp.int32, (1, LANES), 1)
        value = jnp.where(lane < half, value, pltpu.roll(value, half, 1))
        return jnp.concatenate([value] * (total // LANES), axis=1)

    count = spread(counts, total)
    vacant = count == 0
    weight = log_weights[...] - jnp.log(jnp.maximum(count, 1).astype(F32))
    weight = jnp.where(vacant, lay(got[0:1] + got[1:2] + got[2:3]), weight)
    log_det = jnp.where(vacant, lay(got[3:4] + got[4:5]), scalars[0:1, :])
    level = jnp.where(vacant, lay(got[5:6] + got[6:7] + got[7:8]), scalars[1:2, :])
    row = lax.broadcasted_iota(jnp.int32, (TILE, total), 0)
    table = jnp.where(row == 0, log_det, jnp.where(row == 1, level, weight))
    table = jnp.where(row == 3, spread(pairs, total).astype(F32), table)
    mine[...] = jnp.where(row == 4, find(counts, 0).astype(F32), table)


def stats_kernel(even, odd, inverse_temp, own, from_even, from_odd, from_both, updated, stats, marks):
    total = own.shape[1]
    take_even, take_odd = spread(even, total) == 1, spread(odd, total) == 1
    beyond = from_odd[3:4, :] > 0.5

    def settle(r):
        line = slice(r, r + 1)
        swapped = jnp.where(take_even, from_even[line, :], own[line, :])
        return jnp.where(take_odd, jnp.where(beyond, from_both[line, :], from_odd[line, :]), swapped)

    for i, line in enumerate((from_even, from_odd, from_both)):
        marks[0, i] = jnp.max(line[4:5, :]).astype(jnp.int32)
    slots = odd.shape[1]
    slot_of = lax.broadcasted_iota(jnp.int32, (1, total), 1) // (total // slots)
    for i, slot in enumerate(find_two(odd)):
        marks[0, 3 + i] = jnp.max(jnp.where(beyond & (slot_of == slot), 1.0, 0.0)).astype(jnp.int32)
    new = own[2:3, :] + settle(0) - inverse_temp[0] * settle(1)
    updated[...] = new
    peak = jnp.max(new, axis=1, keepdims=True)
    shifted = jnp.exp(new - peak)
    one = jnp.sum(shifted, axis=1, keepdims=True)
    two = jnp.sum(shifted * shifted, axis=1, keepdims=True)
    lane = lax.broadcasted_iota(jnp.int32, stats.shape, 1)
    stats[...] = jnp.where(lane == 0, peak, jnp.where(lane == 1, one, two))


def final_kernel(particle_total, updated, stats, new_weights, ess):
    table = stats[...]
    peaks = table[:, 0:1]
    peak = jnp.max(peaks, axis=0, keepdims=True)
    factor = jnp.exp(peaks - peak)
    one = jnp.sum(table[:, 1:2] * factor, axis=0, keepdims=True) * (1.0 / TILE)
    two = jnp.sum(table[:, 2:3] * factor * factor, axis=0, keepdims=True) * (1.0 / TILE)
    log_one = jnp.log(one)
    new_weights[...] = updated[...] - (peak + log_one)
    count = jnp.log(jnp.full((1, 1), particle_total, F32))
    ess[0] = jnp.max(2.0 * log_one - jnp.log(two) - count)


def at_slot(ref, slot, block_rows):
    return ref.at[pl.ds(pl.multiple_of(slot * block_rows, block_rows), block_rows), :]


def go_all(copies):
    for go, copy in copies:

        @pl.when(go)
        def _():
            copy.start()


def wait_all(copies):
    for go, copy in copies:

        @pl.when(go)
        def _():
            copy.wait()


def next_kernel(even, odd, rows, received, packed, sems):
    block_rows = packed.shape[0] // SWAPS
    slots = even.shape[1]
    pair = find_two(even)
    parts = [slice(i * block_rows, (i + 1) * block_rows) for i in range(SWAPS)]
    copies = []
    odd_pair = find_two(odd)
    for i, slot in enumerate(odd_pair):
        source = at_slot(rows, jnp.minimum(slot, slots - 1), block_rows)
        go = (slot < slots) & (slot != pair[0]) & (slot != pair[1])
        copies.append((go, pltpu.make_async_copy(source, packed.at[parts[i], :], sems.at[i])))
    go_all(copies)
    for i, slot in enumerate(odd_pair):
        for j in range(SWAPS):

            @pl.when((slot < slots) & (slot == pair[j]))
            def _():
                packed[parts[i], :] = received[parts[j], :]

    wait_all(copies)


def join_kernel(
    counts, even, odd, marks, rows_in, filled, late_even, late_odd, late_both, from_even, from_odd, rows, sems
):
    del rows_in
    block_rows = from_even.shape[0] // SWAPS
    width = filled.shape[1]
    slots = counts.shape[1]
    vacant = find(counts, 0)
    pair, odd_pair = find_two(even), find_two(odd)
    copies = []

    def has(chosen, slot):
        return (slot >= 0) & (slot < slots) & ((slot == chosen[0]) | (slot == chosen[1]))

    def spill(go, source, slot, sem):
        to = at_slot(rows, jnp.clip(slot, 0, slots - 1), block_rows)
        for c in range(4):
            part = source.at[c * block_rows : (c + 1) * block_rows, :]
            column = to.at[:, c * width : (c + 1) * width]
            copies.append((go, pltpu.make_async_copy(part, column, sems.at[sem + c])))

    def place(go, source, i, slot, sem):
        part = source.at[i * block_rows : (i + 1) * block_rows, :]
        to = at_slot(rows, jnp.minimum(slot, slots - 1), block_rows)
        copies.append((go, pltpu.make_async_copy(part, to, sems.at[sem])))

    even_vacant, odd_vacant, both_vacant = marks[0, 0], marks[0, 1], marks[0, 2]
    free = jnp.logical_not(has(pair, vacant) | has(odd_pair, vacant))
    spill((vacant >= 0) & free, filled, vacant, 0)
    spill(has(pair, even_vacant) & jnp.logical_not(has(odd_pair, even_vacant)), late_even, even_vacant, 4)
    for i, slot in enumerate(pair):
        go = (slot < slots) & (slot != even_vacant) & jnp.logical_not(has(odd_pair, slot))
        place(go, from_even, i, slot, 16 + i)
    near, far = False, False
    for i, slot in enumerate(odd_pair):
        beyond = marks[0, 3 + i] == 1
        live = slot < slots
        near_hit = live & jnp.logical_not(beyond) & (slot == odd_vacant)
        far_hit = live & beyond & (slot == both_vacant)
        near, far = near | near_hit, far | far_hit
        place(live & jnp.logical_not(near_hit | far_hit), from_odd, i, slot, 16 + SWAPS + i)
    spill(near, late_odd, odd_vacant, 8)
    spill(far, late_both, both_vacant, 12)
    go_all(copies)
    wait_all(copies)


def per_device(
    particles,
    log_weights,
    offspring,
    even_pairs,
    odd_pairs,
    inverse_temp,
    flow_in,
    flow_mid,
    flow_out,
    energy_in,
    energy_mid,
    energy_out,
):
    block_count = offspring.shape[1]
    total, features = particles.shape[1:]
    block_rows = total // block_count
    hidden = flow_mid.shape[0]
    dom_count = lax.axis_size("dom")
    groups = lax.axis_size("temp")
    width = features // 4
    rows = particles.reshape(total, features)
    weights = (flow_in, flow_mid, flow_out, energy_in, energy_mid)
    read_out = energy_out.reshape(1, hidden)
    held_rows = dom_count * TILE
    weight_scratch = [pltpu.VMEM(w.shape, w.dtype) for w in weights]
    shape = jax.ShapeDtypeStruct
    weight_bytes = sum(2 * w.size for w in weights)

    def cost(count):
        flops = 2 * count * (sum(w.size for w in weights) + energy_in.size // 2)
        return pl.CostEstimate(
            flops=flops, transcendentals=count * features * 2, bytes_accessed=weight_bytes
        )

    pieces = pl.pallas_call(
        spare_kernel,
        out_shape=shape((held_rows, width + LANES), BF16),
        in_specs=[SMEM, VMEM, VMEM, ANY] + [ANY] * 5,
        out_specs=VMEM,
        scratch_shapes=[pltpu.VMEM((block_rows, features), BF16)]
        + weight_scratch
        + [pltpu.SemaphoreType.DMA((5,)), pltpu.SemaphoreType.DMA(())],
        cost_estimate=cost(block_rows),
        name="spare",
    )(offspring, log_weights, read_out, rows, *weights)

    def exchange(x):
        cut = x.reshape(dom_count, TILE, x.shape[1])
        cut = lax.all_to_all(cut, "dom", 0, 0, tiled=True)
        return cut.reshape(x.shape)

    def swap(x, pairs):
        return lax.ppermute(x, "temp", pairs)

    held = exchange(pieces)
    pack = shape((SWAPS * block_rows, features), BF16)
    done, scalars, packed = pl.pallas_call(
        rows_kernel,
        out_shape=(shape((total, features), BF16), shape((TILE, total), F32), pack),
        in_specs=[SMEM, VMEM, ANY] + [ANY] * 5,
        out_specs=(ANY, VMEM, VMEM),
        scratch_shapes=weight_scratch
        + [
            pltpu.VMEM((total, features), BF16),
            pltpu.SemaphoreType.DMA((5,)),
            pltpu.SemaphoreType.DMA((2,)),
            pltpu.SemaphoreType.DMA((2,)),
        ],
        cost_estimate=cost(total),
        name="rows",
    )(even_pairs, read_out, rows, *weights)
    even = [(i, i + 1 - 2 * (i % 2)) for i in range(groups)]
    odd = [(i, i - 1 + 2 * (i % 2)) for i in range(1, groups - 1)]
    both = [(even[source][1], target) for source, target in odd]
    from_even_rows = swap(packed, even)
    follow = pl.pallas_call(
        next_kernel,
        out_shape=pack,
        in_specs=[SMEM, SMEM, ANY, VMEM],
        out_specs=VMEM,
        scratch_shapes=[pltpu.SemaphoreType.DMA((SWAPS,))],
        compiler_params=pltpu.CompilerParams(vmem_limit_bytes=8 << 20),
        name="next",
    )
    from_even_rows = inside(from_even_rows)
    packed = follow(even_pairs, odd_pairs, done, from_even_rows)
    from_odd_rows = inside(swap(packed, odd))

    me = lax.axis_index("dom").astype(jnp.int32).reshape(1)
    routed, mine = pl.pallas_call(
        route_kernel,
        out_shape=(shape((held_rows, width), BF16), shape((TILE, total), F32)),
        in_specs=[SMEM, SMEM, SMEM, VMEM, VMEM, VMEM],
        out_specs=(VMEM, VMEM),
        scratch_shapes=[pltpu.VMEM((held_rows, LANES), F32)],
        compiler_params=pltpu.CompilerParams(vmem_limit_bytes=16 << 20),
        name="route",
    )(me, offspring, even_pairs, log_weights, inside(held), scalars)
    filled = exchange(routed)

    from_even = swap(mine, even)
    from_odd = swap(mine, odd)
    from_both = swap(mine, both)
    settle = pl.pallas_call(
        stats_kernel,
        out_shape=(
            shape((1, total), F32),
            shape((held_rows, LANES), F32),
            shape((1, TILE), jnp.int32),
        ),
        in_specs=[SMEM, SMEM, SMEM, VMEM, VMEM, VMEM, VMEM],
        out_specs=(VMEM, VMEM, SMEM),
        compiler_params=pltpu.CompilerParams(vmem_limit_bytes=8 << 20),
        name="stats",
    )
    lines = [inside(line) for line in (from_even, from_odd, from_both)]
    updated, stats, marks = settle(even_pairs, odd_pairs, inverse_temp, mine, *lines)
    stats = exchange(stats)
    close = pl.pallas_call(
        functools.partial(final_kernel, float(total * dom_count)),
        out_shape=(shape((1, total), F32), shape((1,), F32)),
        in_specs=[VMEM, VMEM],
        out_specs=(VMEM, SMEM),
        compiler_params=pltpu.CompilerParams(vmem_limit_bytes=8 << 20),
        name="final",
    )
    new_log_weights, log_ess = close(updated, inside(stats))

    late = [inside(swap(filled, pairs)) for pairs in (even, odd, both)]
    join = pl.pallas_call(
        join_kernel,
        out_shape=shape((total, features), BF16),
        in_specs=[SMEM] * 4 + [ANY] + [VMEM] * 6,
        out_specs=ANY,
        scratch_shapes=[pltpu.SemaphoreType.DMA((16 + 2 * SWAPS,))],
        input_output_aliases={4: 0},
        compiler_params=pltpu.CompilerParams(vmem_limit_bytes=8 << 20),
        name="join",
    )
    done = join(
        offspring,
        even_pairs,
        odd_pairs,
        marks,
        done,
        inside(filled),
        *late,
        from_even_rows,
        from_odd_rows,
    )
    return done.reshape(1, total, features), new_log_weights, log_ess


def solution(mesh):
    in_specs = (
        P("temp", "dom", None),
        P("temp", "dom"),
        P("temp", "dom"),
        P("temp", "dom"),
        P("temp", "dom"),
        P("temp"),
        P(),
        P(),
        P(),
        P(),
        P(),
        P(),
    )
    out_specs = (P("temp", "dom", None), P("temp", "dom"), P("temp"))

    return jax.shard_map(
        per_device, mesh=mesh, in_specs=in_specs, out_specs=out_specs, check_vma=False
    )
```

```python
import functools

import jax
import jax.numpy as jnp
from jax import lax
from jax.experimental import pallas as pl
from jax.experimental.pallas import tpu as pltpu
from jax.sharding import PartitionSpec as P


SWAPS = 2
TILE = 8
LANES = 128

old_level = 0.5
new_level = 0.75
scale_limit = 0.05

F32 = jnp.float32
BF16 = jnp.bfloat16
SMEM = pl.BlockSpec(memory_space=pltpu.SMEM)
VMEM = pl.BlockSpec(memory_space=pltpu.VMEM)
ANY = pl.BlockSpec(memory_space=pl.ANY)


def gelu(x):
    half = 0.5 * x
    inner = x * (0.7978845608028654 + (0.7978845608028654 * 0.044715) * (x * x))
    return half + half * jnp.tanh(inner)


def inside(x):
    return pltpu.with_memory_space_constraint(x, pltpu.VMEM)


def outside(x):
    return pltpu.with_memory_space_constraint(x, pltpu.HBM)


def mul(a, b):
    return jnp.dot(a, b, preferred_element_type=F32)


def find(flags, value):
    slot = jnp.int32(-1)
    for b in range(flags.shape[1]):
        slot = jnp.where(flags[0, b] == value, b, slot)
    return slot


def find_two(flags):
    count = flags.shape[1]
    first, second = jnp.int32(count), jnp.int32(count)
    for b in reversed(range(count)):
        hit = flags[0, b] == 1
        second = jnp.where(hit, first, second)
        first = jnp.where(hit, b, first)
    return first, second


def spread(flags, width):
    count = flags.shape[1]
    slot = lax.broadcasted_iota(jnp.int32, (1, width), 1) // (width // count)
    row = jnp.zeros((1, width), jnp.int32)
    for b in range(count):
        row = jnp.where(slot == b, flags[0, b], row)
    return row


def step_rows(rows, weights, read_out, ready, keep, chunk):
    flow_in, flow_mid, flow_out, energy_in, energy_mid = weights
    half = rows.shape[1] // 2
    kept = rows[:, :half]
    ready(0)
    hidden = gelu(mul(kept, flow_in[...])).astype(BF16)
    ready(1)
    hidden = gelu(mul(hidden, flow_mid[...])).astype(BF16)
    ready(2)
    log_det = jnp.zeros((rows.shape[0], 1), F32)
    parts, olds = [], []
    for at in range(0, half, chunk):
        log_scale = scale_limit * jnp.tanh(mul(hidden, flow_out[:, at : at + chunk]))
        shift = mul(hidden, flow_out[:, half + at : half + at + chunk])
        log_det += jnp.sum(log_scale, axis=1, keepdims=True)
        old = rows[:, half + at : half + at + chunk]
        moved = (old.astype(F32) * jnp.exp(log_scale) + shift).astype(BF16)
        keep(half + at, moved)
        parts.append(moved)
        olds.append(old)
    ready(3)
    base = mul(kept, energy_in[:half, :])
    before = base + mul(jnp.concatenate(olds, axis=1), energy_in[half:, :])
    after = base + mul(jnp.concatenate(parts, axis=1), energy_in[half:, :])
    ready(4)
    levels = []
    for value in (before, after):
        unit = gelu(mul(gelu(value).astype(BF16), energy_mid[...]))
        levels.append(jnp.sum(unit * read_out, axis=1, keepdims=True))
    return log_det, new_level * levels[1] - old_level * levels[0]


def fetches(sources, targets, sems):
    return [
        pltpu.make_async_copy(source, target, sems.at[i])
        for i, (source, target) in enumerate(zip(sources, targets, strict=True))
    ]


def split(value, terms):
    parts = []
    for _ in range(terms):
        part = value.astype(BF16).astype(F32)
        parts.append(part)
        value = value - part
    return parts


def spare_kernel(
    counts, log_weights, read_out, particles, w0, w1, w2, w3, w4, out, rows, s0, s1, s2, s3, s4, sems, row_sem
):
    scratch = (s0, s1, s2, s3, s4)
    copies = fetches((w0, w1, w2, w3, w4), scratch, sems)
    block_rows = rows.shape[0]
    spare, vacant = find(counts, 2), find(counts, 0)
    slot = jnp.maximum(spare, 0)
    own = pltpu.make_async_copy(
        particles.at[pl.ds(pl.multiple_of(slot * block_rows, block_rows), block_rows), :], rows, row_sem
    )
    own.start()
    for copy in copies:
        copy.start()
    own.wait()
    width = rows.shape[1] // 4

    def keep(at, moved):
        done = 0
        while done < moved.shape[1]:
            c, start = divmod(at + done, width)
            size = min(moved.shape[1] - done, width - start)
            out[c * block_rows : (c + 1) * block_rows, start : start + size] = moved[:, done : done + size]
            done += size

    log_det, level = step_rows(
        rows, scratch, read_out[...], lambda i: copies[i].wait(), keep, width
    )
    for c in range(2):
        out[c * block_rows : (c + 1) * block_rows, :width] = rows[:, c * width : (c + 1) * width]
    lane = lax.broadcasted_iota(jnp.int32, (block_rows, LANES), 1)
    table = jnp.where(lane == 0, log_det, jnp.where(lane == 1, level, 0.0))
    table = jnp.concatenate([table] * (LANES // block_rows), axis=0).T
    weight = jnp.zeros((1, LANES), F32)
    for j in range(log_weights.shape[1] // LANES):
        weight = jnp.where(slot // 2 == j, log_weights[:, j * LANES : (j + 1) * LANES], weight)
    weight = jnp.where(slot % 2 == 0, weight, pltpu.roll(weight, LANES // 2, 1))
    weight = weight - jnp.log(jnp.full((1, LANES), 2.0, F32))
    terms = split(weight, 3) + split(table[0:1, :], 2) + split(table[1:2, :], 3)
    row = lax.broadcasted_iota(jnp.int32, (TILE, LANES), 0)
    lane = lax.broadcasted_iota(jnp.int32, (TILE, LANES), 1)
    extra = jnp.zeros((TILE, LANES), F32)
    for i, term in enumerate(terms):
        extra = jnp.where(row == i, term, extra)
    flag = jnp.where(lane < 96, (spare >= 0).astype(F32), (vacant >= 0).astype(F32))
    extra = jnp.where(lane < LANES // 2, extra, flag)
    out[:, width:] = jnp.concatenate([extra] * (out.shape[0] // TILE), axis=0).astype(BF16)


def rows_kernel(
    pairs, read_out, particles, w0, w1, w2, w3, w4, out, scalars, packed, s0, s1, s2, s3, s4, rows, sems, row_sem, out_sem
):
    scratch = (s0, s1, s2, s3, s4)
    copies = fetches((w0, w1, w2, w3, w4), scratch, sems)
    half = rows.shape[1] // 2
    parts = [slice(0, half), slice(half, 2 * half)]
    loads = [pltpu.make_async_copy(particles.at[:, p], rows.at[:, p], row_sem.at[i]) for i, p in enumerate(parts)]
    loads[0].start()
    copies[0].start()
    copies[1].start()
    copies[2].start()
    loads[1].start()
    copies[3].start()
    copies[4].start()

    def ready(i):
        copies[i].wait()
        if i == 2:
            loads[1].wait()

    loads[0].wait()
    kept_out = pltpu.make_async_copy(rows.at[:, parts[0]], out.at[:, parts[0]], out_sem.at[0])
    kept_out.start()

    def keep(at, moved):
        rows[:, at : at + moved.shape[1]] = moved

    log_det, level = step_rows(rows, scratch, read_out[...], ready, keep, 512)
    moved_out = pltpu.make_async_copy(rows.at[:, parts[1]], out.at[:, parts[1]], out_sem.at[1])
    moved_out.start()
    lane = lax.broadcasted_iota(jnp.int32, (rows.shape[0], LANES), 1)
    table = jnp.where(lane == 0, log_det, jnp.where(lane == 1, level, 0.0)).T
    scalars[...] = table[:TILE, :]
    block_rows = packed.shape[0] // SWAPS
    slots = pairs.shape[1]
    for i, slot in enumerate(find_two(pairs)):
        start = pl.multiple_of(jnp.minimum(slot, slots - 1) * block_rows, block_rows)
        packed[i * block_rows : (i + 1) * block_rows, :] = rows[pl.ds(start, block_rows), :]
    kept_out.wait()
    moved_out.wait()


def route_kernel(me, counts, pairs, log_weights, held, scalars, out, mine, tags):
    size = held.shape[0]
    width = out.shape[1]
    tag = held[:, width:]
    flags = tag.astype(F32)
    turned = flags.T
    half, late = LANES // 2, 96
    spare_col, vacant_col = flags[:, half : half + 1], flags[:, late : late + 1]
    spare_row, vacant_row = turned[half : half + 1, :], turned[late : late + 1, :]
    to = lax.broadcasted_iota(jnp.int32, (size, size), 0)
    source = lax.broadcasted_iota(jnp.int32, (size, size), 1)
    to_dev, source_dev = to // TILE, source // TILE
    vacant_rank = jnp.sum(jnp.where(source_dev < to_dev, vacant_row, 0.0), axis=1, keepdims=True)
    spare_rank = jnp.sum(jnp.where(to_dev < source_dev, spare_col, 0.0), axis=0, keepdims=True)
    hit = (vacant_rank == spare_rank) & (to % TILE == source % TILE)
    hit = hit & (vacant_col > 0.5) & (spare_row > 0.5)
    pick = jnp.where(hit, 1.0, 0.0).astype(BF16)
    out[...] = mul(pick, held[:, :width]).astype(BF16)
    tags[...] = mul(pick, tag)
    got = tags[pl.ds(pl.multiple_of(me[0] * TILE, TILE), TILE), :]
    total = log_weights.shape[1]

    def lay(value):
        lane = lax.broadcasted_iota(jnp.int32, (1, LANES), 1)
        value = jnp.where(lane < half, value, pltpu.roll(value, half, 1))
        return jnp.concatenate([value] * (total // LANES), axis=1)

    count = spread(counts, total)
    vacant = count == 0
    weight = log_weights[...] - jnp.log(jnp.maximum(count, 1).astype(F32))
    weight = jnp.where(vacant, lay(got[0:1] + got[1:2] + got[2:3]), weight)
    log_det = jnp.where(vacant, lay(got[3:4] + got[4:5]), scalars[0:1, :])
    level = jnp.where(vacant, lay(got[5:6] + got[6:7] + got[7:8]), scalars[1:2, :])
    row = lax.broadcasted_iota(jnp.int32, (TILE, total), 0)
    table = jnp.where(row == 0, log_det, jnp.where(row == 1, level, weight))
    table = jnp.where(row == 3, spread(pairs, total).astype(F32), table)
    mine[...] = jnp.where(row == 4, find(counts, 0).astype(F32), table)


def stats_kernel(even, odd, inverse_temp, own, from_even, from_odd, from_both, updated, stats, marks):
    total = own.shape[1]
    take_even, take_odd = spread(even, total) == 1, spread(odd, total) == 1
    beyond = from_odd[3:4, :] > 0.5

    def settle(r):
        line = slice(r, r + 1)
        swapped = jnp.where(take_even, from_even[line, :], own[line, :])
        return jnp.where(take_odd, jnp.where(beyond, from_both[line, :], from_odd[line, :]), swapped)

    for i, line in enumerate((from_even, from_odd, from_both)):
        marks[0, i] = jnp.max(line[4:5, :]).astype(jnp.int32)
    slots = odd.shape[1]
    slot_of = lax.broadcasted_iota(jnp.int32, (1, total), 1) // (total // slots)
    for i, slot in enumerate(find_two(odd)):
        marks[0, 3 + i] = jnp.max(jnp.where(beyond & (slot_of == slot), 1.0, 0.0)).astype(jnp.int32)
    new = own[2:3, :] + settle(0) - inverse_temp[0] * settle(1)
    updated[...] = new
    peak = jnp.max(new, axis=1, keepdims=True)
    shifted = jnp.exp(new - peak)
    one = jnp.sum(shifted, axis=1, keepdims=True)
    two = jnp.sum(shifted * shifted, axis=1, keepdims=True)
    lane = lax.broadcasted_iota(jnp.int32, stats.shape, 1)
    stats[...] = jnp.where(lane == 0, peak, jnp.where(lane == 1, one, two))


def final_kernel(particle_total, updated, stats, new_weights, ess):
    table = stats[...]
    peaks = table[:, 0:1]
    peak = jnp.max(peaks, axis=0, keepdims=True)
    factor = jnp.exp(peaks - peak)
    one = jnp.sum(table[:, 1:2] * factor, axis=0, keepdims=True) * (1.0 / TILE)
    two = jnp.sum(table[:, 2:3] * factor * factor, axis=0, keepdims=True) * (1.0 / TILE)
    log_one = jnp.log(one)
    new_weights[...] = updated[...] - (peak + log_one)
    count = jnp.log(jnp.full((1, 1), particle_total, F32))
    ess[0] = jnp.max(2.0 * log_one - jnp.log(two) - count)


def at_slot(ref, slot, block_rows):
    return ref.at[pl.ds(pl.multiple_of(slot * block_rows, block_rows), block_rows), :]


def go_all(copies):
    for go, copy in copies:

        @pl.when(go)
        def _():
            copy.start()


def wait_all(copies):
    for go, copy in copies:

        @pl.when(go)
        def _():
            copy.wait()


def next_kernel(even, odd, rows, received, packed, sems):
    block_rows = packed.shape[0] // SWAPS
    slots = even.shape[1]
    pair = find_two(even)
    parts = [slice(i * block_rows, (i + 1) * block_rows) for i in range(SWAPS)]
    copies = []
    odd_pair = find_two(odd)
    for i, slot in enumerate(odd_pair):
        source = at_slot(rows, jnp.minimum(slot, slots - 1), block_rows)
        go = (slot < slots) & (slot != pair[0]) & (slot != pair[1])
        copies.append((go, pltpu.make_async_copy(source, packed.at[parts[i], :], sems.at[i])))
    go_all(copies)
    for i, slot in enumerate(odd_pair):
        for j in range(SWAPS):

            @pl.when((slot < slots) & (slot == pair[j]))
            def _():
                packed[parts[i], :] = received[parts[j], :]

    wait_all(copies)


def join_kernel(
    counts, even, odd, marks, rows_in, filled, late_even, late_odd, late_both, from_even, from_odd, rows, sems
):
    del rows_in
    block_rows = from_even.shape[0] // SWAPS
    width = filled.shape[1]
    slots = counts.shape[1]
    vacant = find(counts, 0)
    pair, odd_pair = find_two(even), find_two(odd)
    copies = []

    def has(chosen, slot):
        return (slot >= 0) & (slot < slots) & ((slot == chosen[0]) | (slot == chosen[1]))

    def spill(go, source, slot, sem):
        to = at_slot(rows, jnp.clip(slot, 0, slots - 1), block_rows)
        for c in range(4):
            part = source.at[c * block_rows : (c + 1) * block_rows, :]
            column = to.at[:, c * width : (c + 1) * width]
            copies.append((go, pltpu.make_async_copy(part, column, sems.at[sem + c])))

    def place(go, source, i, slot, sem):
        part = source.at[i * block_rows : (i + 1) * block_rows, :]
        to = at_slot(rows, jnp.minimum(slot, slots - 1), block_rows)
        copies.append((go, pltpu.make_async_copy(part, to, sems.at[sem])))

    even_vacant, odd_vacant, both_vacant = marks[0, 0], marks[0, 1], marks[0, 2]
    free = jnp.logical_not(has(pair, vacant) | has(odd_pair, vacant))
    spill((vacant >= 0) & free, filled, vacant, 0)
    spill(has(pair, even_vacant) & jnp.logical_not(has(odd_pair, even_vacant)), late_even, even_vacant, 4)
    for i, slot in enumerate(pair):
        go = (slot < slots) & (slot != even_vacant) & jnp.logical_not(has(odd_pair, slot))
        place(go, from_even, i, slot, 16 + i)
    near, far = False, False
    for i, slot in enumerate(odd_pair):
        beyond = marks[0, 3 + i] == 1
        live = slot < slots
        near_hit = live & jnp.logical_not(beyond) & (slot == odd_vacant)
        far_hit = live & beyond & (slot == both_vacant)
        near, far = near | near_hit, far | far_hit
        place(live & jnp.logical_not(near_hit | far_hit), from_odd, i, slot, 16 + SWAPS + i)
    spill(near, late_odd, odd_vacant, 8)
    spill(far, late_both, both_vacant, 12)
    go_all(copies)
    wait_all(copies)


def per_device(
    particles,
    log_weights,
    offspring,
    even_pairs,
    odd_pairs,
    inverse_temp,
    flow_in,
    flow_mid,
    flow_out,
    energy_in,
    energy_mid,
    energy_out,
):
    block_count = offspring.shape[1]
    total, features = particles.shape[1:]
    block_rows = total // block_count
    hidden = flow_mid.shape[0]
    dom_count = lax.axis_size("dom")
    groups = lax.axis_size("temp")
    width = features // 4
    rows = particles.reshape(total, features)
    weights = (flow_in, flow_mid, flow_out, energy_in, energy_mid)
    read_out = energy_out.reshape(1, hidden)
    held_rows = dom_count * TILE
    weight_scratch = [pltpu.VMEM(w.shape, w.dtype) for w in weights]
    shape = jax.ShapeDtypeStruct
    weight_bytes = sum(2 * w.size for w in weights)

    def cost(count):
        flops = 2 * count * (sum(w.size for w in weights) + energy_in.size // 2)
        return pl.CostEstimate(
            flops=flops, transcendentals=count * features * 2, bytes_accessed=weight_bytes
        )

    pieces = pl.pallas_call(
        spare_kernel,
        out_shape=shape((held_rows, width + LANES), BF16),
        in_specs=[SMEM, VMEM, VMEM, ANY] + [ANY] * 5,
        out_specs=VMEM,
        scratch_shapes=[pltpu.VMEM((block_rows, features), BF16)]
        + weight_scratch
        + [pltpu.SemaphoreType.DMA((5,)), pltpu.SemaphoreType.DMA(())],
        cost_estimate=cost(block_rows),
        name="spare",
    )(offspring, log_weights, read_out, rows, *weights)

    def exchange(x):
        cut = x.reshape(dom_count, TILE, x.shape[1])
        cut = lax.all_to_all(cut, "dom", 0, 0, tiled=True)
        return cut.reshape(x.shape)

    def swap(x, pairs):
        return lax.ppermute(x, "temp", pairs)

    held = exchange(pieces)
    pack = shape((SWAPS * block_rows, features), BF16)
    done, scalars, packed = pl.pallas_call(
        rows_kernel,
        out_shape=(shape((total, features), BF16), shape((TILE, total), F32), pack),
        in_specs=[SMEM, VMEM, ANY] + [ANY] * 5,
        out_specs=(ANY, VMEM, VMEM),
        scratch_shapes=weight_scratch
        + [
            pltpu.VMEM((total, features), BF16),
            pltpu.SemaphoreType.DMA((5,)),
            pltpu.SemaphoreType.DMA((2,)),
            pltpu.SemaphoreType.DMA((2,)),
        ],
        cost_estimate=cost(total),
        name="rows",
    )(even_pairs, read_out, rows, *weights)
    even = [(i, i + 1 - 2 * (i % 2)) for i in range(groups)]
    odd = [(i, i - 1 + 2 * (i % 2)) for i in range(1, groups - 1)]
    both = [(even[source][1], target) for source, target in odd]
    from_even_rows = swap(packed, even)
    follow = pl.pallas_call(
        next_kernel,
        out_shape=pack,
        in_specs=[SMEM, SMEM, ANY, VMEM],
        out_specs=VMEM,
        scratch_shapes=[pltpu.SemaphoreType.DMA((SWAPS,))],
        compiler_params=pltpu.CompilerParams(vmem_limit_bytes=8 << 20),
        name="next",
    )
    from_even_rows = inside(from_even_rows)
    packed = follow(even_pairs, odd_pairs, outside(done), from_even_rows)
    from_odd_rows = inside(swap(packed, odd))

    me = lax.axis_index("dom").astype(jnp.int32).reshape(1)
    routed, mine = pl.pallas_call(
        route_kernel,
        out_shape=(shape((held_rows, width), BF16), shape((TILE, total), F32)),
        in_specs=[SMEM, SMEM, SMEM, VMEM, VMEM, VMEM],
        out_specs=(VMEM, VMEM),
        scratch_shapes=[pltpu.VMEM((held_rows, LANES), F32)],
        compiler_params=pltpu.CompilerParams(vmem_limit_bytes=16 << 20),
        name="route",
    )(me, offspring, even_pairs, log_weights, inside(held), outside(scalars))
    filled = exchange(routed)

    from_even = swap(mine, even)
    from_odd = swap(mine, odd)
    from_both = swap(mine, both)
    settle = pl.pallas_call(
        stats_kernel,
        out_shape=(
            shape((1, total), F32),
            shape((held_rows, LANES), F32),
            shape((1, TILE), jnp.int32),
        ),
        in_specs=[SMEM, SMEM, SMEM, VMEM, VMEM, VMEM, VMEM],
        out_specs=(VMEM, VMEM, SMEM),
        compiler_params=pltpu.CompilerParams(vmem_limit_bytes=8 << 20),
        name="stats",
    )
    lines = [inside(line) for line in (from_even, from_odd, from_both)]
    updated, stats, marks = settle(even_pairs, odd_pairs, inverse_temp, mine, *lines)
    stats = exchange(stats)
    close = pl.pallas_call(
        functools.partial(final_kernel, float(total * dom_count)),
        out_shape=(shape((1, total), F32), shape((1,), F32)),
        in_specs=[VMEM, VMEM],
        out_specs=(VMEM, SMEM),
        compiler_params=pltpu.CompilerParams(vmem_limit_bytes=8 << 20),
        name="final",
    )
    new_log_weights, log_ess = close(updated, inside(stats))

    late = [inside(swap(filled, pairs)) for pairs in (even, odd, both)]
    join = pl.pallas_call(
        join_kernel,
        out_shape=shape((total, features), BF16),
        in_specs=[SMEM] * 4 + [ANY] + [VMEM] * 6,
        out_specs=ANY,
        scratch_shapes=[pltpu.SemaphoreType.DMA((16 + 2 * SWAPS,))],
        input_output_aliases={4: 0},
        compiler_params=pltpu.CompilerParams(vmem_limit_bytes=8 << 20),
        name="join",
    )
    done = join(
        offspring,
        even_pairs,
        odd_pairs,
        marks,
        done,
        inside(filled),
        *late,
        from_even_rows,
        from_odd_rows,
    )
    return done.reshape(1, total, features), new_log_weights, log_ess


def solution(mesh):
    in_specs = (
        P("temp", "dom", None),
        P("temp", "dom"),
        P("temp", "dom"),
        P("temp", "dom"),
        P("temp", "dom"),
        P("temp"),
        P(),
        P(),
        P(),
        P(),
        P(),
        P(),
    )
    out_specs = (P("temp", "dom", None), P("temp", "dom"), P("temp"))

    return jax.shard_map(
        per_device, mesh=mesh, in_specs=in_specs, out_specs=out_specs, check_vma=False
    )
```

```python
import functools

import jax
import jax.numpy as jnp
from jax import lax
from jax.experimental import pallas as pl
from jax.experimental.pallas import tpu as pltpu
from jax.sharding import PartitionSpec as P


SWAPS = 2
TILE = 8
LANES = 128

old_level = 0.5
new_level = 0.75
scale_limit = 0.05

F32 = jnp.float32
BF16 = jnp.bfloat16
SMEM = pl.BlockSpec(memory_space=pltpu.SMEM)
VMEM = pl.BlockSpec(memory_space=pltpu.VMEM)
ANY = pl.BlockSpec(memory_space=pl.ANY)


def gelu(x):
    half = 0.5 * x
    inner = x * (0.7978845608028654 + (0.7978845608028654 * 0.044715) * (x * x))
    return half + half * jnp.tanh(inner)


def inside(x):
    return pltpu.with_memory_space_constraint(x, pltpu.VMEM)


def outside(x):
    return pltpu.with_memory_space_constraint(x, pltpu.HBM)


def mul(a, b):
    return jnp.dot(a, b, preferred_element_type=F32)


def find(flags, value):
    slot = jnp.int32(-1)
    for b in range(flags.shape[1]):
        slot = jnp.where(flags[0, b] == value, b, slot)
    return slot


def find_two(flags):
    count = flags.shape[1]
    first, second = jnp.int32(count), jnp.int32(count)
    for b in reversed(range(count)):
        hit = flags[0, b] == 1
        second = jnp.where(hit, first, second)
        first = jnp.where(hit, b, first)
    return first, second


def spread(flags, width):
    count = flags.shape[1]
    slot = lax.broadcasted_iota(jnp.int32, (1, width), 1) // (width // count)
    row = jnp.zeros((1, width), jnp.int32)
    for b in range(count):
        row = jnp.where(slot == b, flags[0, b], row)
    return row


def step_rows(rows, weights, read_out, ready, keep, chunk):
    flow_in, flow_mid, flow_out, energy_in, energy_mid = weights
    half = rows.shape[1] // 2
    kept = rows[:, :half]
    ready(0)
    hidden = gelu(mul(kept, flow_in[...])).astype(BF16)
    ready(1)
    hidden = gelu(mul(hidden, flow_mid[...])).astype(BF16)
    ready(2)
    log_det = jnp.zeros((rows.shape[0], 1), F32)
    parts, olds = [], []
    for at in range(0, half, chunk):
        log_scale = scale_limit * jnp.tanh(mul(hidden, flow_out[:, at : at + chunk]))
        shift = mul(hidden, flow_out[:, half + at : half + at + chunk])
        log_det += jnp.sum(log_scale, axis=1, keepdims=True)
        old = rows[:, half + at : half + at + chunk]
        moved = (old.astype(F32) * jnp.exp(log_scale) + shift).astype(BF16)
        keep(half + at, moved)
        parts.append(moved)
        olds.append(old)
    ready(3)
    base = mul(kept, energy_in[:half, :])
    before = base + mul(jnp.concatenate(olds, axis=1), energy_in[half:, :])
    after = base + mul(jnp.concatenate(parts, axis=1), energy_in[half:, :])
    ready(4)
    levels = []
    for value in (before, after):
        unit = gelu(mul(gelu(value).astype(BF16), energy_mid[...]))
        levels.append(jnp.sum(unit * read_out, axis=1, keepdims=True))
    return log_det, new_level * levels[1] - old_level * levels[0]


def fetches(sources, targets, sems):
    return [
        pltpu.make_async_copy(source, target, sems.at[i])
        for i, (source, target) in enumerate(zip(sources, targets, strict=True))
    ]


def split(value, terms):
    parts = []
    for _ in range(terms):
        part = value.astype(BF16).astype(F32)
        parts.append(part)
        value = value - part
    return parts


def spare_kernel(
    counts, log_weights, read_out, particles, w0, w1, w2, w3, w4, out, rows, s0, s1, s2, s3, s4, sems, row_sem
):
    scratch = (s0, s1, s2, s3, s4)
    copies = fetches((w0, w1, w2, w3, w4), scratch, sems)
    block_rows = rows.shape[0]
    spare, vacant = find(counts, 2), find(counts, 0)
    slot = jnp.maximum(spare, 0)
    own = pltpu.make_async_copy(
        particles.at[pl.ds(pl.multiple_of(slot * block_rows, block_rows), block_rows), :], rows, row_sem
    )
    own.start()
    for copy in copies[:3]:
        copy.start()
    own.wait()
    width = rows.shape[1] // 4

    def keep(at, moved):
        done = 0
        while done < moved.shape[1]:
            c, start = divmod(at + done, width)
            size = min(moved.shape[1] - done, width - start)
            out[c * block_rows : (c + 1) * block_rows, start : start + size] = moved[:, done : done + size]
            done += size

    def ready(i):
        copies[i].wait()
        if i == 0:
            copies[3].start()
            copies[4].start()

    log_det, level = step_rows(rows, scratch, read_out[...], ready, keep, width)
    for c in range(2):
        out[c * block_rows : (c + 1) * block_rows, :width] = rows[:, c * width : (c + 1) * width]
    lane = lax.broadcasted_iota(jnp.int32, (block_rows, LANES), 1)
    table = jnp.where(lane == 0, log_det, jnp.where(lane == 1, level, 0.0))
    table = jnp.concatenate([table] * (LANES // block_rows), axis=0).T
    weight = jnp.zeros((1, LANES), F32)
    for j in range(log_weights.shape[1] // LANES):
        weight = jnp.where(slot // 2 == j, log_weights[:, j * LANES : (j + 1) * LANES], weight)
    weight = jnp.where(slot % 2 == 0, weight, pltpu.roll(weight, LANES // 2, 1))
    weight = weight - jnp.log(jnp.full((1, LANES), 2.0, F32))
    terms = split(weight, 3) + split(table[0:1, :], 2) + split(table[1:2, :], 3)
    row = lax.broadcasted_iota(jnp.int32, (TILE, LANES), 0)
    lane = lax.broadcasted_iota(jnp.int32, (TILE, LANES), 1)
    extra = jnp.zeros((TILE, LANES), F32)
    for i, term in enumerate(terms):
        extra = jnp.where(row == i, term, extra)
    flag = jnp.where(lane < 96, (spare >= 0).astype(F32), (vacant >= 0).astype(F32))
    extra = jnp.where(lane < LANES // 2, extra, flag)
    out[:, width:] = jnp.concatenate([extra] * (out.shape[0] // TILE), axis=0).astype(BF16)


def rows_kernel(
    pairs, read_out, particles, w0, w1, w2, w3, w4, out, scalars, packed, s0, s1, s2, s3, s4, rows, sems, row_sem, out_sem
):
    scratch = (s0, s1, s2, s3, s4)
    copies = fetches((w0, w1, w2, w3, w4), scratch, sems)
    half = rows.shape[1] // 2
    parts = [slice(0, half), slice(half, 2 * half)]
    loads = [pltpu.make_async_copy(particles.at[:, p], rows.at[:, p], row_sem.at[i]) for i, p in enumerate(parts)]
    loads[0].start()
    copies[0].start()
    copies[1].start()
    copies[2].start()
    loads[1].start()
    copies[3].start()
    copies[4].start()

    def ready(i):
        copies[i].wait()
        if i == 2:
            loads[1].wait()

    loads[0].wait()
    kept_out = pltpu.make_async_copy(rows.at[:, parts[0]], out.at[:, parts[0]], out_sem.at[0])
    kept_out.start()

    def keep(at, moved):
        rows[:, at : at + moved.shape[1]] = moved

    log_det, level = step_rows(rows, scratch, read_out[...], ready, keep, 512)
    moved_out = pltpu.make_async_copy(rows.at[:, parts[1]], out.at[:, parts[1]], out_sem.at[1])
    moved_out.start()
    lane = lax.broadcasted_iota(jnp.int32, (rows.shape[0], LANES), 1)
    table = jnp.where(lane == 0, log_det, jnp.where(lane == 1, level, 0.0)).T
    scalars[...] = table[:TILE, :]
    block_rows = packed.shape[0] // SWAPS
    slots = pairs.shape[1]
    for i, slot in enumerate(find_two(pairs)):
        start = pl.multiple_of(jnp.minimum(slot, slots - 1) * block_rows, block_rows)
        packed[i * block_rows : (i + 1) * block_rows, :] = rows[pl.ds(start, block_rows), :]
    kept_out.wait()
    moved_out.wait()


def route_kernel(me, counts, pairs, log_weights, held, scalars, out, mine, tags):
    size = held.shape[0]
    width = out.shape[1]
    tag = held[:, width:]
    flags = tag.astype(F32)
    turned = flags.T
    half, late = LANES // 2, 96
    spare_col, vacant_col = flags[:, half : half + 1], flags[:, late : late + 1]
    spare_row, vacant_row = turned[half : half + 1, :], turned[late : late + 1, :]
    to = lax.broadcasted_iota(jnp.int32, (size, size), 0)
    source = lax.broadcasted_iota(jnp.int32, (size, size), 1)
    to_dev, source_dev = to // TILE, source // TILE
    vacant_rank = jnp.sum(jnp.where(source_dev < to_dev, vacant_row, 0.0), axis=1, keepdims=True)
    spare_rank = jnp.sum(jnp.where(to_dev < source_dev, spare_col, 0.0), axis=0, keepdims=True)
    hit = (vacant_rank == spare_rank) & (to % TILE == source % TILE)
    hit = hit & (vacant_col > 0.5) & (spare_row > 0.5)
    pick = jnp.where(hit, 1.0, 0.0).astype(BF16)
    out[...] = mul(pick, held[:, :width]).astype(BF16)
    tags[...] = mul(pick, tag)
    got = tags[pl.ds(pl.multiple_of(me[0] * TILE, TILE), TILE), :]
    total = log_weights.shape[1]

    def lay(value):
        lane = lax.broadcasted_iota(jnp.int32, (1, LANES), 1)
        value = jnp.where(lane < half, value, pltpu.roll(value, half, 1))
        return jnp.concatenate([value] * (total // LANES), axis=1)

    count = spread(counts, total)
    vacant = count == 0
    weight = log_weights[...] - jnp.log(jnp.maximum(count, 1).astype(F32))
    weight = jnp.where(vacant, lay(got[0:1] + got[1:2] + got[2:3]), weight)
    log_det = jnp.where(vacant, lay(got[3:4] + got[4:5]), scalars[0:1, :])
    level = jnp.where(vacant, lay(got[5:6] + got[6:7] + got[7:8]), scalars[1:2, :])
    row = lax.broadcasted_iota(jnp.int32, (TILE, total), 0)
    table = jnp.where(row == 0, log_det, jnp.where(row == 1, level, weight))
    mine[...] = jnp.where(row == 3, spread(pairs, total).astype(F32), table)


def stats_kernel(even, odd, inverse_temp, own, from_even, from_odd, from_both, updated, stats):
    total = own.shape[1]
    take_even, take_odd = spread(even, total) == 1, spread(odd, total) == 1
    beyond = from_odd[3:4, :] > 0.5

    def settle(r):
        line = slice(r, r + 1)
        swapped = jnp.where(take_even, from_even[line, :], own[line, :])
        return jnp.where(take_odd, jnp.where(beyond, from_both[line, :], from_odd[line, :]), swapped)

    new = own[2:3, :] + settle(0) - inverse_temp[0] * settle(1)
    updated[...] = new
    peak = jnp.max(new, axis=1, keepdims=True)
    shifted = jnp.exp(new - peak)
    one = jnp.sum(shifted, axis=1, keepdims=True)
    two = jnp.sum(shifted * shifted, axis=1, keepdims=True)
    lane = lax.broadcasted_iota(jnp.int32, stats.shape, 1)
    stats[...] = jnp.where(lane == 0, peak, jnp.where(lane == 1, one, two))


def final_kernel(particle_total, updated, stats, new_weights, ess):
    table = stats[...]
    peaks = table[:, 0:1]
    peak = jnp.max(peaks, axis=0, keepdims=True)
    factor = jnp.exp(peaks - peak)
    one = jnp.sum(table[:, 1:2] * factor, axis=0, keepdims=True) * (1.0 / TILE)
    two = jnp.sum(table[:, 2:3] * factor * factor, axis=0, keepdims=True) * (1.0 / TILE)
    log_one = jnp.log(one)
    new_weights[...] = updated[...] - (peak + log_one)
    count = jnp.log(jnp.full((1, 1), particle_total, F32))
    ess[0] = jnp.max(2.0 * log_one - jnp.log(two) - count)


def at_slot(ref, slot, block_rows):
    return ref.at[pl.ds(pl.multiple_of(slot * block_rows, block_rows), block_rows), :]


def join_kernel(
    counts, other_counts, even, odd, rows_in, filled, filled_other, received, later, rows, packed, sems
):
    del rows_in, later
    block_rows = packed.shape[0] // SWAPS
    width = filled.shape[1]
    slots = counts.shape[1]
    vacant, other_vacant = find(counts, 0), find(other_counts, 0)
    pair, odd_pair = find_two(even), find_two(odd)
    parts = [slice(i * block_rows, (i + 1) * block_rows) for i in range(SWAPS)]
    copies = []

    def spill(go, source, slot, sem):
        to = at_slot(rows, jnp.clip(slot, 0, slots - 1), block_rows)
        for c in range(4):
            part = source.at[c * block_rows : (c + 1) * block_rows, :]
            column = to.at[:, c * width : (c + 1) * width]
            copies.append((go, pltpu.make_async_copy(part, column, sems.at[sem + c])))

    def hold(go, source, i):
        @pl.when(go)
        def _():
            for c in range(4):
                packed[parts[i], c * width : (c + 1) * width] = source[c * block_rows : (c + 1) * block_rows, :]

    spill((vacant >= 0) & (vacant != pair[0]) & (vacant != pair[1]), filled, vacant, 0)
    spill((other_vacant >= 0) & ((other_vacant == pair[0]) | (other_vacant == pair[1])), filled_other, other_vacant, 4)
    for i, slot in enumerate(pair):
        to = at_slot(rows, jnp.minimum(slot, slots - 1), block_rows)
        go = (slot < slots) & (slot != other_vacant)
        copies.append((go, pltpu.make_async_copy(received.at[parts[i], :], to, sems.at[8 + i])))
    for i, slot in enumerate(odd_pair):
        swapped = (slot == pair[0]) | (slot == pair[1])
        source = at_slot(rows, jnp.minimum(slot, slots - 1), block_rows)
        go = (slot < slots) & (slot != vacant) & jnp.logical_not(swapped)
        copies.append((go, pltpu.make_async_copy(source, packed.at[parts[i], :], sems.at[8 + SWAPS + i])))
    for go, copy in copies:

        @pl.when(go)
        def _():
            copy.start()

    for i, slot in enumerate(odd_pair):
        swapped = (slot == pair[0]) | (slot == pair[1])
        hold((slot == vacant) & jnp.logical_not(swapped), filled, i)
        hold((slot < slots) & swapped & (slot == other_vacant), filled_other, i)
        for j in range(SWAPS):

            @pl.when((slot < slots) & (slot == pair[j]) & (slot != other_vacant))
            def _():
                packed[parts[i], :] = received[parts[j], :]

    for go, copy in copies:

        @pl.when(go)
        def _():
            copy.wait()


def last_kernel(flags, rows_in, received, rows, sems):
    del rows_in
    block_rows = received.shape[0] // SWAPS
    slots = flags.shape[1]
    copies = []
    for i, slot in enumerate(find_two(flags)):
        source = received.at[i * block_rows : (i + 1) * block_rows, :]
        to = at_slot(rows, jnp.minimum(slot, slots - 1), block_rows)
        copies.append((slot < slots, pltpu.make_async_copy(source, to, sems.at[i])))
    for go, copy in copies:

        @pl.when(go)
        def _():
            copy.start()

    for go, copy in copies:

        @pl.when(go)
        def _():
            copy.wait()


def per_device(
    particles,
    log_weights,
    offspring,
    even_pairs,
    odd_pairs,
    inverse_temp,
    flow_in,
    flow_mid,
    flow_out,
    energy_in,
    energy_mid,
    energy_out,
):
    block_count = offspring.shape[1]
    total, features = particles.shape[1:]
    block_rows = total // block_count
    hidden = flow_mid.shape[0]
    dom_count = lax.axis_size("dom")
    groups = lax.axis_size("temp")
    width = features // 4
    rows = particles.reshape(total, features)
    weights = (flow_in, flow_mid, flow_out, energy_in, energy_mid)
    read_out = energy_out.reshape(1, hidden)
    held_rows = dom_count * TILE
    weight_scratch = [pltpu.VMEM(w.shape, w.dtype) for w in weights]
    shape = jax.ShapeDtypeStruct
    weight_bytes = sum(2 * w.size for w in weights)

    def cost(count):
        flops = 2 * count * (sum(w.size for w in weights) + energy_in.size // 2)
        return pl.CostEstimate(
            flops=flops, transcendentals=count * features * 2, bytes_accessed=weight_bytes
        )

    pieces = pl.pallas_call(
        spare_kernel,
        out_shape=shape((held_rows, width + LANES), BF16),
        in_specs=[SMEM, VMEM, VMEM, ANY] + [ANY] * 5,
        out_specs=VMEM,
        scratch_shapes=[pltpu.VMEM((block_rows, features), BF16)]
        + weight_scratch
        + [pltpu.SemaphoreType.DMA((5,)), pltpu.SemaphoreType.DMA(())],
        cost_estimate=cost(block_rows),
        name="spare",
    )(offspring, log_weights, read_out, rows, *weights)

    def exchange(x):
        cut = x.reshape(dom_count, TILE, x.shape[1])
        cut = lax.all_to_all(cut, "dom", 0, 0, tiled=True)
        return cut.reshape(x.shape)

    def swap(x, pairs):
        return lax.ppermute(x, "temp", pairs)

    held = exchange(pieces)
    pack = shape((SWAPS * block_rows, features), BF16)
    done, scalars, packed = pl.pallas_call(
        rows_kernel,
        out_shape=(shape((total, features), BF16), shape((TILE, total), F32), pack),
        in_specs=[SMEM, VMEM, ANY] + [ANY] * 5,
        out_specs=(ANY, VMEM, VMEM),
        scratch_shapes=weight_scratch
        + [
            pltpu.VMEM((total, features), BF16),
            pltpu.SemaphoreType.DMA((5,)),
            pltpu.SemaphoreType.DMA((2,)),
            pltpu.SemaphoreType.DMA((2,)),
        ],
        cost_estimate=cost(total),
        name="rows",
    )(even_pairs, read_out, rows, *weights)
    even = [(i, i + 1 - 2 * (i % 2)) for i in range(groups)]
    odd = [(i, i - 1 + 2 * (i % 2)) for i in range(1, groups - 1)]
    both = [(even[source][1], target) for source, target in odd]
    received = swap(packed, even)
    other_counts = swap(offspring, even)

    me = lax.axis_index("dom").astype(jnp.int32).reshape(1)
    routed, mine = pl.pallas_call(
        route_kernel,
        out_shape=(shape((held_rows, width), BF16), shape((TILE, total), F32)),
        in_specs=[SMEM, SMEM, SMEM, VMEM, VMEM, VMEM],
        out_specs=(VMEM, VMEM),
        scratch_shapes=[pltpu.VMEM((held_rows, LANES), F32)],
        compiler_params=pltpu.CompilerParams(vmem_limit_bytes=16 << 20),
        name="route",
    )(me, offspring, even_pairs, log_weights, inside(held), outside(scalars))
    filled = exchange(routed)

    from_even = swap(mine, even)
    from_odd = swap(mine, odd)
    from_both = swap(mine, both)
    settle = pl.pallas_call(
        stats_kernel,
        out_shape=(shape((1, total), F32), shape((held_rows, LANES), F32)),
        in_specs=[SMEM, SMEM, SMEM, VMEM, VMEM, VMEM, VMEM],
        out_specs=(VMEM, VMEM),
        compiler_params=pltpu.CompilerParams(vmem_limit_bytes=8 << 20),
        name="stats",
    )
    lines = [inside(line) for line in (from_even, from_odd, from_both)]
    updated, stats = settle(even_pairs, odd_pairs, inverse_temp, mine, *lines)
    stats = exchange(stats)
    close = pl.pallas_call(
        functools.partial(final_kernel, float(total * dom_count)),
        out_shape=(shape((1, total), F32), shape((1,), F32)),
        in_specs=[VMEM, VMEM],
        out_specs=(VMEM, SMEM),
        compiler_params=pltpu.CompilerParams(vmem_limit_bytes=8 << 20),
        name="final",
    )
    new_log_weights, log_ess = close(updated, inside(stats))

    whole = shape((total, features), BF16)
    filled_other = swap(filled, even)
    done, packed = pl.pallas_call(
        join_kernel,
        out_shape=(whole, pack),
        in_specs=[SMEM] * 4 + [ANY] + [VMEM] * 3 + [ANY],
        out_specs=(ANY, VMEM),
        scratch_shapes=[pltpu.SemaphoreType.DMA((8 + 2 * SWAPS,))],
        input_output_aliases={4: 0},
        compiler_params=pltpu.CompilerParams(vmem_limit_bytes=8 << 20),
        name="join",
    )(
        offspring,
        other_counts,
        even_pairs,
        odd_pairs,
        outside(done),
        inside(filled),
        inside(filled_other),
        inside(received),
        updated,
    )
    received = swap(packed, odd)
    done = pl.pallas_call(
        last_kernel,
        out_shape=whole,
        in_specs=[SMEM, ANY, VMEM],
        out_specs=ANY,
        scratch_shapes=[pltpu.SemaphoreType.DMA((SWAPS,))],
        input_output_aliases={1: 0},
        compiler_params=pltpu.CompilerParams(vmem_limit_bytes=8 << 20),
        name="odd",
    )(odd_pairs, outside(done), inside(received))
    return done.reshape(1, total, features), new_log_weights, log_ess


def solution(mesh):
    in_specs = (
        P("temp", "dom", None),
        P("temp", "dom"),
        P("temp", "dom"),
        P("temp", "dom"),
        P("temp", "dom"),
        P("temp"),
        P(),
        P(),
        P(),
        P(),
        P(),
        P(),
    )
    out_specs = (P("temp", "dom", None), P("temp", "dom"), P("temp"))

    return jax.shard_map(per_device, mesh=mesh, in_specs=in_specs, out_specs=out_specs, check_vma=False)
```

```python
import functools

import jax
import jax.numpy as jnp
from jax import lax
from jax.experimental import pallas as pl
from jax.experimental.pallas import tpu as pltpu
from jax.sharding import PartitionSpec as P


SWAPS = 2
TILE = 8
LANES = 128

old_level = 0.5
new_level = 0.75
scale_limit = 0.05

F32 = jnp.float32
BF16 = jnp.bfloat16
SMEM = pl.BlockSpec(memory_space=pltpu.SMEM)
VMEM = pl.BlockSpec(memory_space=pltpu.VMEM)
ANY = pl.BlockSpec(memory_space=pl.ANY)


def gelu(x):
    half = 0.5 * x
    inner = x * (0.7978845608028654 + (0.7978845608028654 * 0.044715) * (x * x))
    return half + half * jnp.tanh(inner)


def inside(x):
    return pltpu.with_memory_space_constraint(x, pltpu.VMEM)


def outside(x):
    return pltpu.with_memory_space_constraint(x, pltpu.HBM)


def mul(a, b):
    return jnp.dot(a, b, preferred_element_type=F32)


def find(flags, value):
    slot = jnp.int32(-1)
    for b in range(flags.shape[1]):
        slot = jnp.where(flags[0, b] == value, b, slot)
    return slot


def find_two(flags):
    count = flags.shape[1]
    first, second = jnp.int32(count), jnp.int32(count)
    for b in reversed(range(count)):
        hit = flags[0, b] == 1
        second = jnp.where(hit, first, second)
        first = jnp.where(hit, b, first)
    return first, second


def spread(flags, width):
    count = flags.shape[1]
    slot = lax.broadcasted_iota(jnp.int32, (1, width), 1) // (width // count)
    row = jnp.zeros((1, width), jnp.int32)
    for b in range(count):
        row = jnp.where(slot == b, flags[0, b], row)
    return row


def step_rows(rows, weights, read_out, ready, keep, chunk):
    flow_in, flow_mid, flow_out, energy_in, energy_mid = weights
    half = rows.shape[1] // 2
    kept = rows[:, :half]
    ready(0)
    hidden = gelu(mul(kept, flow_in[...])).astype(BF16)
    ready(1)
    hidden = gelu(mul(hidden, flow_mid[...])).astype(BF16)
    ready(2)
    log_det = jnp.zeros((rows.shape[0], 1), F32)
    parts, olds = [], []
    for at in range(0, half, chunk):
        log_scale = scale_limit * jnp.tanh(mul(hidden, flow_out[:, at : at + chunk]))
        shift = mul(hidden, flow_out[:, half + at : half + at + chunk])
        log_det += jnp.sum(log_scale, axis=1, keepdims=True)
        old = rows[:, half + at : half + at + chunk]
        moved = (old.astype(F32) * jnp.exp(log_scale) + shift).astype(BF16)
        keep(half + at, moved)
        parts.append(moved)
        olds.append(old)
    ready(3)
    base = mul(kept, energy_in[:half, :])
    before = base + mul(jnp.concatenate(olds, axis=1), energy_in[half:, :])
    after = base + mul(jnp.concatenate(parts, axis=1), energy_in[half:, :])
    ready(4)
    levels = []
    for value in (before, after):
        unit = gelu(mul(gelu(value).astype(BF16), energy_mid[...]))
        levels.append(jnp.sum(unit * read_out, axis=1, keepdims=True))
    return log_det, new_level * levels[1] - old_level * levels[0]


def fetches(sources, targets, sems):
    return [
        pltpu.make_async_copy(source, target, sems.at[i])
        for i, (source, target) in enumerate(zip(sources, targets, strict=True))
    ]


def split(value, terms):
    parts = []
    for _ in range(terms):
        part = value.astype(BF16).astype(F32)
        parts.append(part)
        value = value - part
    return parts


def spare_kernel(
    counts_in, log_weights_in, read_out_in, particles, w0, w1, w2, w3, w4,
    out, rows, s0, s1, s2, s3, s4, counts, log_weights, read_out, sems, row_sem, small_sem
):
    scratch = (s0, s1, s2, s3, s4)
    copies = fetches((w0, w1, w2, w3, w4), scratch, sems)
    small = fetches((counts_in, log_weights_in, read_out_in), (counts, log_weights, read_out), small_sem)
    for copy in (*small, *copies[:3]):
        copy.start()
    block_rows = rows.shape[0]
    small[0].wait()
    spare, vacant = find(counts, 2), find(counts, 0)
    slot = jnp.maximum(spare, 0)
    own = pltpu.make_async_copy(
        particles.at[pl.ds(pl.multiple_of(slot * block_rows, block_rows), block_rows), :], rows, row_sem
    )
    own.start()
    own.wait()
    small[1].wait()
    small[2].wait()
    width = rows.shape[1] // 4

    def keep(at, moved):
        done = 0
        while done < moved.shape[1]:
            c, start = divmod(at + done, width)
            size = min(moved.shape[1] - done, width - start)
            out[c * block_rows : (c + 1) * block_rows, start : start + size] = moved[:, done : done + size]
            done += size

    def ready(i):
        copies[i].wait()
        if i == 0:
            copies[3].start()
            copies[4].start()

    log_det, level = step_rows(rows, scratch, read_out[...], ready, keep, width)
    for c in range(2):
        out[c * block_rows : (c + 1) * block_rows, :width] = rows[:, c * width : (c + 1) * width]
    lane = lax.broadcasted_iota(jnp.int32, (block_rows, LANES), 1)
    table = jnp.where(lane == 0, log_det, jnp.where(lane == 1, level, 0.0))
    table = jnp.concatenate([table] * (LANES // block_rows), axis=0).T
    weight = jnp.zeros((1, LANES), F32)
    for j in range(log_weights.shape[1] // LANES):
        weight = jnp.where(slot // 2 == j, log_weights[:, j * LANES : (j + 1) * LANES], weight)
    weight = jnp.where(slot % 2 == 0, weight, pltpu.roll(weight, LANES // 2, 1))
    weight = weight - jnp.log(jnp.full((1, LANES), 2.0, F32))
    terms = split(weight, 3) + split(table[0:1, :], 2) + split(table[1:2, :], 3)
    row = lax.broadcasted_iota(jnp.int32, (TILE, LANES), 0)
    lane = lax.broadcasted_iota(jnp.int32, (TILE, LANES), 1)
    extra = jnp.zeros((TILE, LANES), F32)
    for i, term in enumerate(terms):
        extra = jnp.where(row == i, term, extra)
    flag = jnp.where(lane < 96, (spare >= 0).astype(F32), (vacant >= 0).astype(F32))
    extra = jnp.where(lane < LANES // 2, extra, flag)
    out[:, width:] = jnp.concatenate([extra] * (out.shape[0] // TILE), axis=0).astype(BF16)


def rows_kernel(
    pairs, read_out, particles, w0, w1, w2, w3, w4, out, scalars, packed, s0, s1, s2, s3, s4, rows, sems, row_sem, out_sem
):
    scratch = (s0, s1, s2, s3, s4)
    copies = fetches((w0, w1, w2, w3, w4), scratch, sems)
    half = rows.shape[1] // 2
    parts = [slice(0, half), slice(half, 2 * half)]
    loads = [pltpu.make_async_copy(particles.at[:, p], rows.at[:, p], row_sem.at[i]) for i, p in enumerate(parts)]
    loads[0].start()
    copies[0].start()
    copies[1].start()
    copies[2].start()
    loads[1].start()
    copies[3].start()
    copies[4].start()

    def ready(i):
        copies[i].wait()
        if i == 2:
            loads[1].wait()

    loads[0].wait()
    kept_out = pltpu.make_async_copy(rows.at[:, parts[0]], out.at[:, parts[0]], out_sem.at[0])
    kept_out.start()

    def keep(at, moved):
        rows[:, at : at + moved.shape[1]] = moved

    log_det, level = step_rows(rows, scratch, read_out[...], ready, keep, 512)
    moved_out = pltpu.make_async_copy(rows.at[:, parts[1]], out.at[:, parts[1]], out_sem.at[1])
    moved_out.start()
    lane = lax.broadcasted_iota(jnp.int32, (rows.shape[0], LANES), 1)
    table = jnp.where(lane == 0, log_det, jnp.where(lane == 1, level, 0.0)).T
    scalars[...] = table[:TILE, :]
    block_rows = packed.shape[0] // SWAPS
    slots = pairs.shape[1]
    for i, slot in enumerate(find_two(pairs)):
        start = pl.multiple_of(jnp.minimum(slot, slots - 1) * block_rows, block_rows)
        packed[i * block_rows : (i + 1) * block_rows, :] = rows[pl.ds(start, block_rows), :]
    kept_out.wait()
    moved_out.wait()


def route_kernel(held, out, tags):
    size = held.shape[0]
    width = out.shape[1]
    tag = held[:, width:]
    flags = tag.astype(F32)
    turned = flags.T
    half, late = LANES // 2, 96
    spare_col, vacant_col = flags[:, half : half + 1], flags[:, late : late + 1]
    spare_row, vacant_row = turned[half : half + 1, :], turned[late : late + 1, :]
    to = lax.broadcasted_iota(jnp.int32, (size, size), 0)
    source = lax.broadcasted_iota(jnp.int32, (size, size), 1)
    to_dev, source_dev = to // TILE, source // TILE
    vacant_rank = jnp.sum(jnp.where(source_dev < to_dev, vacant_row, 0.0), axis=1, keepdims=True)
    spare_rank = jnp.sum(jnp.where(to_dev < source_dev, spare_col, 0.0), axis=0, keepdims=True)
    hit = (vacant_rank == spare_rank) & (to % TILE == source % TILE)
    hit = hit & (vacant_col > 0.5) & (spare_row > 0.5)
    pick = jnp.where(hit, 1.0, 0.0).astype(BF16)
    out[...] = mul(pick, held[:, :width]).astype(BF16)
    tags[...] = mul(pick, tag)


def lines_kernel(me, counts, pairs, log_weights, tags, scalars, mine):
    half = LANES // 2
    got = tags[pl.ds(pl.multiple_of(me[0] * TILE, TILE), TILE), :]
    total = log_weights.shape[1]

    def lay(value):
        lane = lax.broadcasted_iota(jnp.int32, (1, LANES), 1)
        value = jnp.where(lane < half, value, pltpu.roll(value, half, 1))
        return jnp.concatenate([value] * (total // LANES), axis=1)

    count = spread(counts, total)
    vacant = count == 0
    weight = log_weights[...] - jnp.log(jnp.maximum(count, 1).astype(F32))
    weight = jnp.where(vacant, lay(got[0:1] + got[1:2] + got[2:3]), weight)
    log_det = jnp.where(vacant, lay(got[3:4] + got[4:5]), scalars[0:1, :])
    level = jnp.where(vacant, lay(got[5:6] + got[6:7] + got[7:8]), scalars[1:2, :])
    row = lax.broadcasted_iota(jnp.int32, (TILE, total), 0)
    table = jnp.where(row == 0, log_det, jnp.where(row == 1, level, weight))
    mine[...] = jnp.where(row == 3, spread(pairs, total).astype(F32), table)


def stats_kernel(even, odd, inverse_temp, own, from_even, from_odd, from_both, updated, stats):
    total = own.shape[1]
    take_even, take_odd = spread(even, total) == 1, spread(odd, total) == 1
    beyond = from_odd[3:4, :] > 0.5

    def settle(r):
        line = slice(r, r + 1)
        swapped = jnp.where(take_even, from_even[line, :], own[line, :])
        return jnp.where(take_odd, jnp.where(beyond, from_both[line, :], from_odd[line, :]), swapped)

    new = own[2:3, :] + settle(0) - inverse_temp[0] * settle(1)
    updated[...] = new
    peak = jnp.max(new, axis=1, keepdims=True)
    shifted = jnp.exp(new - peak)
    one = jnp.sum(shifted, axis=1, keepdims=True)
    two = jnp.sum(shifted * shifted, axis=1, keepdims=True)
    lane = lax.broadcasted_iota(jnp.int32, stats.shape, 1)
    stats[...] = jnp.where(lane == 0, peak, jnp.where(lane == 1, one, two))


def final_kernel(particle_total, updated, stats, new_weights, ess):
    table = stats[...]
    peaks = table[:, 0:1]
    peak = jnp.max(peaks, axis=0, keepdims=True)
    factor = jnp.exp(peaks - peak)
    one = jnp.sum(table[:, 1:2] * factor, axis=0, keepdims=True) * (1.0 / TILE)
    two = jnp.sum(table[:, 2:3] * factor * factor, axis=0, keepdims=True) * (1.0 / TILE)
    log_one = jnp.log(one)
    new_weights[...] = updated[...] - (peak + log_one)
    count = jnp.log(jnp.full((1, 1), particle_total, F32))
    ess[0] = jnp.max(2.0 * log_one - jnp.log(two) - count)


def at_slot(ref, slot, block_rows):
    return ref.at[pl.ds(pl.multiple_of(slot * block_rows, block_rows), block_rows), :]


def join_kernel(
    counts, other_counts, even, odd, rows_in, filled, filled_other, received, later, rows, packed, sems
):
    del rows_in, later
    block_rows = packed.shape[0] // SWAPS
    width = filled.shape[1]
    slots = counts.shape[1]
    vacant, other_vacant = find(counts, 0), find(other_counts, 0)
    pair, odd_pair = find_two(even), find_two(odd)
    parts = [slice(i * block_rows, (i + 1) * block_rows) for i in range(SWAPS)]
    copies = []

    def spill(go, source, slot, sem):
        to = at_slot(rows, jnp.clip(slot, 0, slots - 1), block_rows)
        for c in range(4):
            part = source.at[c * block_rows : (c + 1) * block_rows, :]
            column = to.at[:, c * width : (c + 1) * width]
            copies.append((go, pltpu.make_async_copy(part, column, sems.at[sem + c])))

    def hold(go, source, i):
        @pl.when(go)
        def _():
            for c in range(4):
                packed[parts[i], c * width : (c + 1) * width] = source[c * block_rows : (c + 1) * block_rows, :]

    spill((vacant >= 0) & (vacant != pair[0]) & (vacant != pair[1]), filled, vacant, 0)
    spill((other_vacant >= 0) & ((other_vacant == pair[0]) | (other_vacant == pair[1])), filled_other, other_vacant, 4)
    for i, slot in enumerate(pair):
        to = at_slot(rows, jnp.minimum(slot, slots - 1), block_rows)
        go = (slot < slots) & (slot != other_vacant)
        copies.append((go, pltpu.make_async_copy(received.at[parts[i], :], to, sems.at[8 + i])))
    for i, slot in enumerate(odd_pair):
        swapped = (slot == pair[0]) | (slot == pair[1])
        source = at_slot(rows, jnp.minimum(slot, slots - 1), block_rows)
        go = (slot < slots) & (slot != vacant) & jnp.logical_not(swapped)
        copies.append((go, pltpu.make_async_copy(source, packed.at[parts[i], :], sems.at[8 + SWAPS + i])))
    for go, copy in copies:

        @pl.when(go)
        def _():
            copy.start()

    for i, slot in enumerate(odd_pair):
        swapped = (slot == pair[0]) | (slot == pair[1])
        hold((slot == vacant) & jnp.logical_not(swapped), filled, i)
        hold((slot < slots) & swapped & (slot == other_vacant), filled_other, i)
        for j in range(SWAPS):

            @pl.when((slot < slots) & (slot == pair[j]) & (slot != other_vacant))
            def _():
                packed[parts[i], :] = received[parts[j], :]

    for go, copy in copies:

        @pl.when(go)
        def _():
            copy.wait()


def last_kernel(flags, rows_in, received, rows, sems):
    del rows_in
    block_rows = received.shape[0] // SWAPS
    slots = flags.shape[1]
    copies = []
    for i, slot in enumerate(find_two(flags)):
        source = received.at[i * block_rows : (i + 1) * block_rows, :]
        to = at_slot(rows, jnp.minimum(slot, slots - 1), block_rows)
        copies.append((slot < slots, pltpu.make_async_copy(source, to, sems.at[i])))
    for go, copy in copies:

        @pl.when(go)
        def _():
            copy.start()

    for go, copy in copies:

        @pl.when(go)
        def _():
            copy.wait()


def per_device(
    particles,
    log_weights,
    offspring,
    even_pairs,
    odd_pairs,
    inverse_temp,
    flow_in,
    flow_mid,
    flow_out,
    energy_in,
    energy_mid,
    energy_out,
):
    block_count = offspring.shape[1]
    total, features = particles.shape[1:]
    block_rows = total // block_count
    hidden = flow_mid.shape[0]
    dom_count = lax.axis_size("dom")
    groups = lax.axis_size("temp")
    width = features // 4
    rows = particles.reshape(total, features)
    weights = (flow_in, flow_mid, flow_out, energy_in, energy_mid)
    read_out = energy_out.reshape(1, hidden)
    held_rows = dom_count * TILE
    weight_scratch = [pltpu.VMEM(w.shape, w.dtype) for w in weights]
    shape = jax.ShapeDtypeStruct
    weight_bytes = sum(2 * w.size for w in weights)

    def cost(count):
        flops = 2 * count * (sum(w.size for w in weights) + energy_in.size // 2)
        return pl.CostEstimate(
            flops=flops, transcendentals=count * features * 2, bytes_accessed=weight_bytes
        )

    pieces = pl.pallas_call(
        spare_kernel,
        out_shape=shape((held_rows, width + LANES), BF16),
        in_specs=[ANY] * 9,
        out_specs=VMEM,
        scratch_shapes=[pltpu.VMEM((block_rows, features), BF16)]
        + weight_scratch
        + [
            pltpu.SMEM(offspring.shape, offspring.dtype),
            pltpu.VMEM(log_weights.shape, F32),
            pltpu.VMEM(read_out.shape, F32),
            pltpu.SemaphoreType.DMA((5,)),
            pltpu.SemaphoreType.DMA(()),
            pltpu.SemaphoreType.DMA((3,)),
        ],
        cost_estimate=cost(block_rows),
        name="spare",
    )(offspring, log_weights, read_out, rows, *weights)

    def exchange(x):
        cut = x.reshape(dom_count, TILE, x.shape[1])
        cut = lax.all_to_all(cut, "dom", 0, 0, tiled=True)
        return cut.reshape(x.shape)

    def swap(x, pairs):
        return lax.ppermute(x, "temp", pairs)

    held = exchange(pieces)
    pack = shape((SWAPS * block_rows, features), BF16)
    done, scalars, packed = pl.pallas_call(
        rows_kernel,
        out_shape=(shape((total, features), BF16), shape((TILE, total), F32), pack),
        in_specs=[SMEM, VMEM, ANY] + [ANY] * 5,
        out_specs=(ANY, VMEM, VMEM),
        scratch_shapes=weight_scratch
        + [
            pltpu.VMEM((total, features), BF16),
            pltpu.SemaphoreType.DMA((5,)),
            pltpu.SemaphoreType.DMA((2,)),
            pltpu.SemaphoreType.DMA((2,)),
        ],
        cost_estimate=cost(total),
        name="rows",
    )(even_pairs, read_out, rows, *weights)
    even = [(i, i + 1 - 2 * (i % 2)) for i in range(groups)]
    odd = [(i, i - 1 + 2 * (i % 2)) for i in range(1, groups - 1)]
    both = [(even[source][1], target) for source, target in odd]
    received = swap(packed, even)
    other_counts = swap(offspring, even)

    me = lax.axis_index("dom").astype(jnp.int32).reshape(1)
    routed, tags = pl.pallas_call(
        route_kernel,
        out_shape=(shape((held_rows, width), BF16), shape((held_rows, LANES), F32)),
        in_specs=[VMEM],
        out_specs=(VMEM, VMEM),
        compiler_params=pltpu.CompilerParams(vmem_limit_bytes=16 << 20),
        name="route",
    )(inside(held))
    lay = pl.pallas_call(
        lines_kernel,
        out_shape=shape((TILE, total), F32),
        in_specs=[SMEM, SMEM, SMEM, VMEM, VMEM, VMEM],
        out_specs=VMEM,
        compiler_params=pltpu.CompilerParams(vmem_limit_bytes=8 << 20),
        name="lines",
    )
    mine = lay(me, offspring, even_pairs, log_weights, tags, outside(scalars))
    filled = exchange(routed)

    from_even = swap(mine, even)
    from_odd = swap(mine, odd)
    from_both = swap(mine, both)
    settle = pl.pallas_call(
        stats_kernel,
        out_shape=(shape((1, total), F32), shape((held_rows, LANES), F32)),
        in_specs=[SMEM, SMEM, SMEM, VMEM, VMEM, VMEM, VMEM],
        out_specs=(VMEM, VMEM),
        compiler_params=pltpu.CompilerParams(vmem_limit_bytes=8 << 20),
        name="stats",
    )
    lines = [inside(line) for line in (from_even, from_odd, from_both)]
    updated, stats = settle(even_pairs, odd_pairs, inverse_temp, mine, *lines)
    stats = exchange(stats)
    close = pl.pallas_call(
        functools.partial(final_kernel, float(total * dom_count)),
        out_shape=(shape((1, total), F32), shape((1,), F32)),
        in_specs=[VMEM, VMEM],
        out_specs=(VMEM, SMEM),
        compiler_params=pltpu.CompilerParams(vmem_limit_bytes=8 << 20),
        name="final",
    )
    new_log_weights, log_ess = close(updated, inside(stats))

    whole = shape((total, features), BF16)
    filled_other = swap(filled, even)
    done, packed = pl.pallas_call(
        join_kernel,
        out_shape=(whole, pack),
        in_specs=[SMEM] * 4 + [ANY] + [VMEM] * 3 + [ANY],
        out_specs=(ANY, VMEM),
        scratch_shapes=[pltpu.SemaphoreType.DMA((8 + 2 * SWAPS,))],
        input_output_aliases={4: 0},
        compiler_params=pltpu.CompilerParams(vmem_limit_bytes=8 << 20),
        name="join",
    )(
        offspring,
        other_counts,
        even_pairs,
        odd_pairs,
        outside(done),
        inside(filled),
        inside(filled_other),
        inside(received),
        updated,
    )
    received = swap(packed, odd)
    done = pl.pallas_call(
        last_kernel,
        out_shape=whole,
        in_specs=[SMEM, ANY, VMEM],
        out_specs=ANY,
        scratch_shapes=[pltpu.SemaphoreType.DMA((SWAPS,))],
        input_output_aliases={1: 0},
        compiler_params=pltpu.CompilerParams(vmem_limit_bytes=8 << 20),
        name="odd",
    )(odd_pairs, outside(done), inside(received))
    return done.reshape(1, total, features), new_log_weights, log_ess


def solution(mesh):
    in_specs = (
        P("temp", "dom", None),
        P("temp", "dom"),
        P("temp", "dom"),
        P("temp", "dom"),
        P("temp", "dom"),
        P("temp"),
        P(),
        P(),
        P(),
        P(),
        P(),
        P(),
    )
    out_specs = (P("temp", "dom", None), P("temp", "dom"), P("temp"))

    return jax.shard_map(
        per_device, mesh=mesh, in_specs=in_specs, out_specs=out_specs, check_vma=False
    )
```
